32 devices in a mesh: grp: 2 (over x), date: 16 (over z, y, core).
Axes of the slice: x: 2, y: 2, z: 4, core: 2. Of those that a mesh axis runs over, the one named last changes fastest.
Arguments:
- radar_stack: bfloat16 [2, 128, 256, 256], P(None, 'date', 'grp'), parts along dimension 2, may hold values from -6 to 6
- filter_taps: float32 [2, 128, 128], P(None, 'date'), may hold values from -0.6 to 0.6
- filter_lengths: int32 [128], P('date'), may hold values from 64 to 128
- resample_kernel: float32 [4], replicated, may hold values from 0.2 to 1
- tile_owner: int32 [512, 1], P(('grp', 'date')), parts along dimension 0, may hold values from 0 to 15; in each aligned block of 16 rows (0 to 15, 16 to 31, ...) at most 2 rows name the same one
- map_slot: int32 [512], P(('grp', 'date')), parts along dimension 0, may hold values from 0 to 7
- correlation: int32 [512], P(('grp', 'date')), parts along dimension 0, may hold values from 1 to 128
- offsets: int32 [512], P(('grp', 'date')), parts along dimension 0, may hold values from 0 to 127
Outputs:
- geocoded: float32 [256, 256, 128], P(('grp', 'date')), parts along dimension 0
The draws below stay inside these ranges and needn't reach their ends.
There are 2 independent parts, one for each index of `grp`. The reference program is written for one: setup_inputs(seed, part) draws one part's arguments, and reference() takes and returns one part's arrays. A program takes and returns all parts, laid end to end along the dimension named above; an argument that names none is the same for every part. Nothing has to cross between parts.
Inputs may be any that keep to these rules, and one draw needn't show every extreme that they name: `tile_owner`: among the 16 tiles of one device, at most 2 name the same owner.
All inputs are finite; a program needn't handle non-finite values. Where the reference program divides by a largest or mean magnitude, that divisor is 1e-20 or more.
Results may differ from the reference program's by a relative error of at most 0.0055.
Values may be sent and summed in bfloat16 or wider, within the bound.
A program may use at most 64 MiB of HBM per device.

```python
import math
import jax
import jax.numpy as jnp
import numpy as np
from jax import lax

DATES = 128
TAPS = 128
RG = 256
PATCH_AZ = 8
PATCH_RG = 16
SWEEPS = 3
TILE = 128
KW = 4
CAP = 2
MAP_DEV = 8
AZ = 128
TILES_DEV = 16
TILES = 256
MAP_TILES = 128
N_DATE = 16


def place_ends(array, key, least, largest):
    extent = array.shape
    index_at = [jax.random.randint(jax.random.fold_in(key, axis), (), 0, extent[axis]) for axis in range(len(extent))]
    array = array.at[tuple(index_at)].set(least)
    longest = extent.index(max(extent))
    index_at[longest] = (index_at[longest] + 1) % extent[longest]
    return array.at[tuple(index_at)].set(largest)


def level_of(stream_key, extent, shards, smallest, largest):
    loudness, own = 1.0, jax.random.fold_in(stream_key, 6)
    for dim, shards_of in shards:
        draws = jnp.exp(jax.random.uniform(jax.random.fold_in(own, dim), (shards_of,), jnp.float32, smallest / len(shards), largest / len(shards)))
        loudness = loudness * jnp.repeat(draws, extent[dim] // shards_of).reshape([-1 if axis == dim else 1 for axis in range(len(extent))])
    return loudness


def assign_block(own_key, own, number, rows, amount, top, most, slope):
    ranking = jax.random.permutation(own_key, amount)
    packed, common = shares(amount, rows * top, most, slope, True), shares(amount, rows * top, most, slope, False)
    places = jnp.arange(amount)

    def named(sizes, turn):
        used = int((sizes > 0).sum())
        fixed = max(1, used // 4)
        passed = fixed + (places - fixed + turn * (used - fixed)) % max(1, amount - fixed)
        return jnp.zeros((amount,), jnp.int32).at[ranking[jnp.where(places < fixed, places, passed)]].set(jnp.asarray(sizes, jnp.int32))

    sizes = jnp.where(number % 4 == 0, named(packed, number // 4), named(common, number - number // 4 - 1))
    mixed = jax.random.permutation(jax.random.fold_in(own, 3), amount)
    source_of, taker = mixed[0:amount // 2 * 2:2], mixed[1:amount // 2 * 2:2]
    room = jnp.minimum(sizes[source_of] - 1, most - sizes[taker]) // 2
    room = jnp.where((source_of == ranking[0]) | (taker == ranking[0]) | (sizes[taker] == 0), 0, jnp.maximum(room, 0))
    passed = jax.random.randint(jax.random.fold_in(own, 4), (amount // 2,), 0, 1 << 20) % (room + 1)
    sizes = sizes.at[source_of].add(-passed).at[taker].add(passed)
    items = jnp.searchsorted(jnp.cumsum(sizes), jnp.arange(rows * top), side="right").astype(jnp.int32)
    listing = items.reshape(top, rows).T
    listing = listing[jax.random.permutation(jax.random.fold_in(own, 1), rows)]
    turn = jax.random.randint(jax.random.fold_in(own, 2), (rows, 1), 0, top)
    return jnp.take_along_axis(listing, (jnp.arange(top)[None, :] + turn) % top, axis=1)


def shares(number_of, total, reach, lean, full):
    loads = [(1 << 20) // math.isqrt(rank ** lean) + 1 for rank in range(1, number_of + 1)]
    largest = reach if full else min(reach, max(-(-total // number_of), total * loads[0] // sum(loads)))
    least = 1 if total - largest >= number_of - 1 else 0
    given, rest = [largest] + [least] * (number_of - 1), total - largest - least * (number_of - 1)
    while rest > 0:
        candidates = [i for i in range(1, number_of) if given[i] < largest] or [i for i in range(1, number_of) if given[i] < reach]
        mass, remaining = sum([loads[i] for i in candidates]), rest
        for i in candidates:
            more = min(reach - given[i], max(1, remaining * loads[i] // mass), rest)
            given[i] = given[i] + more
            rest = rest - more
    return np.array(given)


def gaussian(key, shape, scale, bound, cuts=(), kind=jnp.bfloat16):
    drawn = scale * jax.random.normal(key, shape, jnp.float32)
    if cuts:
        drawn = drawn * level_of(key, shape, cuts, -0.22, 0.18)
    return jnp.clip(drawn, -bound, bound).astype(kind)


def setup_inputs(seed: int = 0, part: int = 0) -> dict:
    streams_of = jax.random.split(jax.random.key(seed), 9)
    part_keys = jax.random.split(jax.random.fold_in(streams_of[8], part), 9)
    radar_stack = gaussian(part_keys[0], (2, DATES, AZ, RG), 1.0, 6.0, ((1, 16),))
    filter_taps = gaussian(streams_of[1], (2, DATES, TAPS), 0.1, 0.6, ((1, 16),), jnp.float32)
    filter_lengths = place_ends(jax.random.randint(streams_of[2], (DATES,), TAPS // 2, TAPS + 1), jax.random.fold_in(streams_of[2], 1), TAPS // 2, TAPS).astype(jnp.int32)
    resample_kernel = jnp.clip(jax.random.uniform(streams_of[3], (KW,), jnp.float32, 0.2, 1.0), 0.2, 1.0)
    tile_owner_keys = jax.random.split(jax.random.fold_in(part_keys[4], 1), TILES // TILES_DEV)
    tile_owner_turns = jax.random.permutation(jax.random.fold_in(part_keys[4], 3), TILES // TILES_DEV)
    tile_owner = jax.vmap(lambda own, number: assign_block(jax.random.fold_in(part_keys[4], 2), own, number, TILES_DEV, N_DATE, 1, CAP, 2))(tile_owner_keys, tile_owner_turns).reshape((TILES, 1))
    map_slot = place_ends(jax.random.randint(part_keys[5], (TILES,), 0, MAP_DEV), jax.random.fold_in(part_keys[5], 1), 0, MAP_DEV - 1).astype(jnp.int32)
    correlation = place_ends(jax.random.randint(part_keys[6], (TILES,), 1, TILE + 1), jax.random.fold_in(part_keys[6], 1), 1, TILE).astype(jnp.int32)
    offsets = place_ends(jax.random.randint(part_keys[7], (TILES,), 0, TILE), jax.random.fold_in(part_keys[7], 1), 0, TILE - 1).astype(jnp.int32)
    return {"radar_stack": radar_stack, "filter_taps": filter_taps, "filter_lengths": filter_lengths, "resample_kernel": resample_kernel, "tile_owner": tile_owner, "map_slot": map_slot, "correlation": correlation, "offsets": offsets}


diag_load = 0.5
small_eps = 1e-05
highest = lax.Precision.HIGHEST

def toeplitz_matrix(taps_one, length_one, rows_count):
    positions = jnp.arange(TAPS, dtype=jnp.int32)
    masked = jnp.where(positions < length_one, taps_one, jnp.zeros_like(taps_one))
    period = 2 * rows_count - 1
    padded = jnp.pad(masked, (0, period - TAPS))
    wrapped = jnp.roll(padded, -(TAPS // 2))
    flat_rows = jnp.tile(wrapped, rows_count)[:rows_count * (period - 1)]
    return flat_rows.reshape(rows_count, period - 1)[:, :rows_count]

def block_operator(taps_date, length_one, rows_count):
    real_mat = toeplitz_matrix(taps_date[0], length_one, rows_count)
    imag_mat = toeplitz_matrix(taps_date[1], length_one, rows_count)
    upper = jnp.concatenate([real_mat, -imag_mat], axis=1)
    lower = jnp.concatenate([imag_mat, real_mat], axis=1)
    return jnp.concatenate([upper, lower], axis=0).astype(jnp.bfloat16)

def complex_product(left_re, left_im, right_re, right_im):

    def mult(first, second):
        return jnp.einsum('pij,pjk->pik', first, second, precision=highest)
    return (mult(left_re, right_re) - mult(left_im, right_im), mult(left_re, right_im) + mult(left_im, right_re))

def whiten_patches(patches):
    values = patches.astype(jnp.float32)
    z_re = values[:, 0]
    z_im = values[:, 1]
    date_count = patches.shape[2]
    look_count = patches.shape[3]
    gram_re = (jnp.einsum('pil,pjl->pij', z_re, z_re, precision=highest) + jnp.einsum('pil,pjl->pij', z_im, z_im, precision=highest)) / look_count
    gram_im = (jnp.einsum('pil,pjl->pij', z_im, z_re, precision=highest) - jnp.einsum('pil,pjl->pij', z_re, z_im, precision=highest)) / look_count
    diagonal = jnp.diagonal(gram_re, axis1=1, axis2=2)
    scaled = lax.rsqrt(diagonal + small_eps)
    outer_scale = scaled[:, :, None] * scaled[:, None, :]
    identity = jnp.eye(date_count, dtype=jnp.float32)
    coher_re = gram_re * outer_scale + diag_load * identity[None]
    coher_im = gram_im * outer_scale
    row_bound = lax.optimization_barrier(jnp.max(lax.optimization_barrier(jnp.sum(jnp.abs(coher_re) + jnp.abs(coher_im), axis=2)), axis=1))
    inverse_re = identity[None] / row_bound[:, None, None]
    inverse_im = jnp.zeros_like(coher_im)
    for _ in range(SWEEPS):
        prod_re, prod_im = complex_product(coher_re, coher_im, inverse_re, inverse_im)
        corr_re, corr_im = complex_product(inverse_re, inverse_im, prod_re, prod_im)
        inverse_re = 2.0 * inverse_re - corr_re
        inverse_im = 2.0 * inverse_im - corr_im
    white_re, white_im = complex_product(inverse_re, inverse_im, z_re, z_im)
    return jnp.stack([white_re, white_im], axis=1).astype(jnp.bfloat16)

def to_patches(field):
    date_count = field.shape[1]
    rows_count = field.shape[2]
    ranges_count = field.shape[3]
    blocks = field.reshape(2, date_count, rows_count // PATCH_AZ, PATCH_AZ, ranges_count // PATCH_RG, PATCH_RG)
    return blocks.transpose(2, 4, 0, 1, 3, 5).reshape(-1, 2, date_count, PATCH_AZ * PATCH_RG)

def from_patches(patches, rows_count, ranges_count):
    date_count = patches.shape[2]
    blocks = patches.reshape(rows_count // PATCH_AZ, ranges_count // PATCH_RG, 2, date_count, PATCH_AZ, PATCH_RG)
    return blocks.transpose(2, 3, 0, 4, 1, 5).reshape(2, date_count, rows_count, ranges_count)

def to_tiles(field):
    date_count = field.shape[1]
    rows_count = field.shape[2]
    ranges_count = field.shape[3]
    blocks = field.reshape(2, date_count, rows_count, ranges_count // TILE, TILE)
    return blocks.transpose(2, 3, 0, 1, 4).reshape(-1, 2 * date_count, TILE)

def resample_tiles(tiles, shifts, resample_kernel):
    rounded = lax.optimization_barrier(resample_kernel.astype(jnp.bfloat16)).astype(jnp.float32)
    column = jnp.arange(TILE, dtype=jnp.int32)
    first_cell = column[None, :] + shifts.astype(jnp.int32)[:, None]
    matrix = jnp.zeros((shifts.shape[0], TILE, TILE), jnp.float32)
    for tap_index in range(KW):
        source = (first_cell + tap_index) % TILE
        matrix = matrix + rounded[tap_index] * (column[None, None, :] == source[:, :, None]).astype(jnp.float32)
    return jnp.einsum('sji,sci->scj', matrix, tiles.astype(jnp.float32), precision=highest)

def reference(radar_stack, filter_taps, filter_lengths, resample_kernel, tile_owner, map_slot, correlation, offsets):
    rows_count = radar_stack.shape[2]
    ranges_count = radar_stack.shape[3]

    def filter_one(operands):
        taps_date, length_one, columns = operands
        operator = block_operator(taps_date, length_one, rows_count).astype(jnp.float32)
        flat_cols = columns.reshape(2 * rows_count, ranges_count).astype(jnp.float32)
        product = jnp.dot(operator, flat_cols, precision=highest)
        return product.reshape(2, rows_count, ranges_count).astype(jnp.bfloat16)
    filtered = lax.map(filter_one, (filter_taps.transpose(1, 0, 2), filter_lengths, radar_stack.transpose(1, 0, 2, 3)))
    filtered = filtered.transpose(1, 0, 2, 3)
    patches = to_patches(filtered)
    grouped = patches.reshape((N_DATE, -1) + patches.shape[1:])
    whitened = lax.map(whiten_patches, grouped).reshape(patches.shape)
    field = from_patches(whitened, rows_count, ranges_count)
    tiles = to_tiles(field)
    tile_count = tiles.shape[0]
    resampled = resample_tiles(tiles, offsets, resample_kernel).reshape(tile_count, -1)
    targets = tile_owner[:, 0] * MAP_DEV + map_slot
    map_iota = jnp.arange(MAP_TILES, dtype=jnp.int32)
    spread = jnp.where(targets[None, :] == map_iota[:, None], correlation.astype(jnp.float32)[None, :], jnp.zeros((), jnp.float32))
    total = jnp.dot(spread, resampled, precision=highest)
    denominator = jnp.maximum(lax.optimization_barrier(jnp.sum(spread, axis=1)), 1.0)
    return (total / denominator[:, None]).reshape(MAP_TILES, 2 * DATES, TILE)
```

```python
from functools import partial

import jax
import jax.numpy as jnp
from jax import lax
from jax.experimental import pallas as pl
from jax.experimental.pallas import tpu as pltpu
from jax.sharding import PartitionSpec as P

PATCH_AZ = 8
PATCH_RG = 16
TILE = 128
KW = 4
MAP_DEV = 8
LANES = 128
PHASES = 2
TOGETHER = 4
GROUPS = 2
CHUNKS = 4
FACTS = 8
SWEEPS = 3

diag_load = 0.5
small_eps = 1e-05
MESH = pl.DeviceIdType.MESH
VMEM = pl.BlockSpec(memory_space=pltpu.VMEM)
HBM = pl.BlockSpec(memory_space=pltpu.MemorySpace.HBM)
BIG = 32 * 1024 * 1024


def whiten_window(zt):
    looks, dates = zt.shape[0], zt.shape[1] // 2
    gram = lax.dot_general(zt, zt, (((0,), (0,)), ((), ())), preferred_element_type=jnp.float32)
    gram_re = (gram[:dates, :dates] + gram[dates:, dates:]) * (1.0 / looks)
    gram_im = (gram[dates:, :dates] - gram[:dates, dates:]) * (1.0 / looks)
    eye = lax.broadcasted_iota(jnp.int32, (dates, dates), 0) == lax.broadcasted_iota(
        jnp.int32, (dates, dates), 1
    )
    diagonal = jnp.where(eye, gram_re, 0.0)
    scale_col = lax.rsqrt(jnp.sum(diagonal, axis=1, keepdims=True) + small_eps)
    scale_row = lax.rsqrt(jnp.sum(diagonal, axis=0, keepdims=True) + small_eps)
    outer = scale_col * scale_row
    coher_re = gram_re * outer + jnp.where(eye, diag_load, 0.0)
    coher_im = gram_im * outer
    sums = jnp.sum(jnp.abs(coher_re) + jnp.abs(coher_im), axis=1, keepdims=True)
    over = 1.0 / jnp.max(sums, axis=0, keepdims=True)

    part_re, part_im = coher_re * over, coher_im * over
    w, rounded = zt.astype(jnp.float32), zt
    for stage in range(SWEEPS):
        re, im = part_re.astype(jnp.bfloat16), part_im.astype(jnp.bfloat16)
        top = jnp.concatenate([re, -im], axis=1)
        whole = jnp.concatenate([top, jnp.concatenate([im, re], axis=1)], axis=0)
        if stage < SWEEPS - 1:
            both = jnp.dot(jnp.concatenate([top, rounded], axis=0), whole, preferred_element_type=jnp.float32)
            part_re = 2.0 * part_re - both[:dates, :dates]
            part_im = 2.0 * part_im + both[:dates, dates:]
            applied = both[dates:]
        else:
            applied = jnp.dot(rounded, whole, preferred_element_type=jnp.float32)
        w = 2.0 * w - applied
        rounded = w.astype(jnp.bfloat16)
    return (w * over).astype(jnp.bfloat16)


def flow_kernel(n, *refs):
    inputs, refs = refs[:8], refs[8:]
    result_ref, cells_ref, got_cells, facts_ref, got_facts, cell_ref, z_ref, white_ref, flat_ref = refs[:9]
    row_msg, got_rows, sums_ref, sum_msg, got_sums, operator_ref, spread_ref, bits_ref, inv_ref = refs[9:18]
    local, refs = refs[18:26], refs[26:]
    len_ref, kern_ref, radar_ref, taps_ref = local[:4]
    fact_refs = local[4:8]
    own_sem, fact_send, fact_recv, cell_send, cell_recv, row_send, row_recv, sum_send, sum_recv, load_sem = refs
    me = lax.axis_index("date")
    dates_here, rows = radar_ref.shape[1], radar_ref.shape[2]
    taps, tile_count = taps_ref.shape[2], fact_refs[0].shape[1]
    total = n * dates_here
    half = LANES // PHASES
    windows = LANES // PATCH_RG
    near = n // GROUPS
    group, rank = me // near, me % near
    tiles = near * tile_count
    deep = 2 * total // near // CHUNKS

    barrier = pltpu.get_barrier_semaphore()
    loads = [pltpu.make_async_copy(x, y, load_sem.at[i]) for i, (x, y) in enumerate(zip(inputs, local))]
    for load in loads:
        load.start()
    for k in range(1, n):
        pl.semaphore_signal(barrier, inc=1, device_id={"date": lax.rem(me + k, n)}, device_id_type=MESH)
    own = [pltpu.make_async_copy(cells_ref.at[h, me], got_cells.at[h, me], own_sem.at[h]) for h in range(PHASES)]

    def remote(src, dst, send, recv, peer):
        return pltpu.make_async_remote_copy(
            src_ref=src, dst_ref=dst, send_sem=send, recv_sem=recv, device_id={"date": peer}, device_id_type=MESH
        )

    def fact_copy(peer, origin):
        return remote(facts_ref, got_facts.at[origin], fact_send.at[peer], fact_recv.at[origin], peer)

    def cell_copy(h, peer, origin):
        return remote(
            cells_ref.at[h, peer], got_cells.at[h, origin], cell_send.at[h, peer], cell_recv.at[h, origin], peer
        )

    def row_copy(h, q, peer, origin):
        to, come = peer % near, origin % near
        return remote(
            row_msg.at[h, to, q], got_rows.at[h, come, q], row_send.at[h, q, to], row_recv.at[h, q, come], peer
        )

    def sum_copy(q, peer, origin):
        return remote(
            sum_msg.at[q, peer], got_sums.at[q, origin], sum_send.at[q, peer], sum_recv.at[q, origin], peer
        )

    def partner(k):
        peer, bit = me, 1
        while bit < n:
            peer = peer + (k // bit) % 2 * (1 - (me // bit) % 2 * 2) * bit
            bit *= 2
        return peer

    def turn(i):
        return n - 1 - i // 2 - i % 2 * (n // 2)

    peers = [turn(i) for i in range(n - 1)]
    inner = list(range(near - 1, 0, -1))

    for load in loads:
        load.wait()
    position = lax.broadcasted_iota(jnp.int32, (1, taps), 1)
    a_iota = lax.broadcasted_iota(jnp.int32, (rows, rows), 0)
    b_iota = lax.broadcasted_iota(jnp.int32, (rows, rows), 1)
    tap_at = b_iota - a_iota + taps // 2
    inside = jnp.logical_and(tap_at >= 0, tap_at < taps)
    low = lax.broadcasted_iota(jnp.int32, (2 * rows, LANES), 1) < half

    def toeplitz(d, which):
        kept = jnp.where(position < len_ref[d], taps_ref[which, pl.ds(d, 1), :], 0.0)
        rolled = pltpu.roll(jnp.broadcast_to(kept, (rows, taps)), taps // 2, 1, stride=1, stride_axis=0)
        return jnp.where(inside, jnp.concatenate([rolled] * (rows // taps), axis=1), 0.0)

    for h in range(PHASES):
        for d in range(dates_here):
            if h == 0:
                t_re, t_im = toeplitz(d, 0), toeplitz(d, 1)
                operator_ref[d] = jnp.concatenate(
                    [jnp.concatenate([t_re, -t_im], axis=1), jnp.concatenate([t_im, t_re], axis=1)], axis=0
                ).astype(jnp.bfloat16)
            columns = jnp.concatenate([radar_ref[0, d], radar_ref[1, d]], axis=0).astype(jnp.float32)
            sides = [columns[:, c * LANES : (c + 1) * LANES] for c in range(2)]
            sides[1 - h] = pltpu.roll(sides[1 - h], half, 1)
            product = jnp.dot(
                operator_ref[d],
                jnp.where(low, sides[0], sides[1]).astype(jnp.bfloat16),
                preferred_element_type=jnp.float32,
            )
            for p in range(n):
                for part in range(2):
                    top = part * rows + p * PATCH_AZ
                    cell_ref[p, pl.ds(part * PATCH_AZ * dates_here + d, PATCH_AZ, stride=dates_here), :] = product[
                        top : top + PATCH_AZ
                    ]
        for p in range(n):
            cells_ref[h, p] = cell_ref[p].astype(jnp.bfloat16)
        if h == 0:
            pl.semaphore_wait(barrier, n - 1)
        for k in peers:
            cell_copy(h, partner(k), me).start()
        own[h].start()

    tile_at = lax.broadcasted_iota(jnp.int32, (LANES, tiles), 0)
    lane_at = lax.broadcasted_iota(jnp.int32, (LANES, tiles), 1)
    placed = (tile_at & 1) * (tiles // 2) + rank * PATCH_AZ + (tile_at >> 1)
    moving = jnp.where(jnp.logical_and(lane_at == placed, tile_at < tile_count), 1.0, 0.0).astype(jnp.bfloat16)
    listed = jnp.concatenate([fact[...] for fact in fact_refs], axis=0).astype(jnp.float32)
    listed = jnp.concatenate([listed, jnp.zeros((FACTS - 4, tile_count), jnp.float32)], axis=0)
    listed = jnp.concatenate([listed, jnp.zeros((FACTS, LANES - tile_count), jnp.float32)], axis=1)
    facts_ref[...] = jnp.dot(listed.astype(jnp.bfloat16), moving, preferred_element_type=jnp.float32)
    for k in peers:
        fact_copy(partner(k), me).start()
    got_facts[me] = facts_ref[...]
    for k in peers:
        fact_copy(partner(k), partner(k)).wait_recv()

    here = got_facts[group * near]
    for s in range(1, near):
        here = here + got_facts[group * near + s]
    target = here[0:1] * MAP_DEV + here[1:2]
    map_at = lax.broadcasted_iota(jnp.int32, (n * MAP_DEV, tiles), 0).astype(jnp.float32)
    spread_ref[...] = jnp.where(map_at == target, here[3:4], 0.0).astype(jnp.bfloat16)
    for j in range(tiles // LANES):
        shift = jnp.broadcast_to(here[2:3, j * LANES : (j + 1) * LANES], (LANES, LANES)).T.astype(jnp.int32)
        for b in range(bits_ref.shape[0]):
            bits_ref[b, j * LANES : (j + 1) * LANES] = (shift >> b) & 1
    mine = me * MAP_DEV + lax.broadcasted_iota(jnp.int32, (MAP_DEV, tiles), 0)
    count = jnp.zeros((MAP_DEV, tiles), jnp.float32)
    for k in range(GROUPS):
        facts = got_facts[k * near]
        for s in range(1, near):
            facts = facts + got_facts[k * near + s]
        count = count + jnp.where(mine.astype(jnp.float32) == facts[0:1] * MAP_DEV + facts[1:2], facts[3:4], 0.0)
    inv_ref[...] = jnp.broadcast_to(
        1.0 / jnp.maximum(jnp.sum(count, axis=1, keepdims=True), 1.0), inv_ref.shape
    )

    per_half = windows // 2
    for h in range(PHASES):
        own[h].wait()
        for k in peers:
            cell_copy(h, partner(k), partner(k)).wait_recv()
        for s in range(n):
            cell_ref[s] = got_cells[h, s].astype(jnp.float32)
        for part in range(2):
            for a in range(PATCH_AZ):
                at = pl.ds((part * PATCH_AZ + a) * dates_here, dates_here)
                line = jnp.concatenate([cell_ref[s, at, :] for s in range(n)], axis=0).T.astype(jnp.bfloat16)
                for j in range(windows):
                    z_ref[j, a * PATCH_RG : (a + 1) * PATCH_RG, part * total : (part + 1) * total] = line[
                        j * PATCH_RG : (j + 1) * PATCH_RG
                    ]

        def whiten(i, carry):
            for q in range(TOGETHER):
                w = i * TOGETHER + q
                white = whiten_window(z_ref[w])
                for a in range(PATCH_AZ):
                    white_ref[a, pl.ds(w * PATCH_RG, PATCH_RG), :] = white[a * PATCH_RG : (a + 1) * PATCH_RG]
            return carry

        lax.fori_loop(0, windows // TOGETHER, whiten, 0)

        for a in range(PATCH_AZ):
            tall = white_ref[a].astype(jnp.float32)
            for part in range(2):
                flat_ref[pl.ds(part * total * PATCH_AZ + a, total, stride=PATCH_AZ), :] = tall[
                    :, part * total : (part + 1) * total
                ].T
        for q in range(CHUNKS):
            for to in range(near):
                row_msg[h, to, q] = flat_ref[
                    pl.ds((to * CHUNKS + q) * deep * PATCH_AZ, deep * PATCH_AZ), :
                ].astype(jnp.bfloat16)
            got_rows[h, rank, q] = row_msg[h, rank, q]
            for k in inner:
                row_copy(h, q, partner(k), me).start()

    first_half = lax.broadcasted_iota(jnp.int32, (tiles // 2, LANES), 1) < half

    def reduce(q, carry):
        for k in inner:
            for h in range(PHASES):
                row_copy(h, q, partner(k), partner(k)).wait_recv()

        def pair(i, carry):
            at = pl.ds(pl.multiple_of(i * 2 * PATCH_AZ, 2 * PATCH_AZ), 2 * PATCH_AZ)
            both = [[got_rows[h, s, q, at, :].astype(jnp.float32) for s in range(near)] for h in range(PHASES)]
            wide = []
            for r in range(2):
                one, two = [
                    jnp.concatenate([x[r * PATCH_AZ : (r + 1) * PATCH_AZ] for x in both[h]], axis=0) for h in range(2)
                ]
                y = jnp.concatenate(
                    [
                        jnp.where(first_half, one, pltpu.roll(two, half, 1)),
                        jnp.where(first_half, pltpu.roll(one, half, 1), two),
                    ],
                    axis=0,
                )
                for b in range(bits_ref.shape[0]):
                    y = jnp.where(bits_ref[b] != 0, pltpu.roll(y, LANES - (1 << b), 1), y)
                wide.append(y.astype(jnp.bfloat16))
            out = jnp.dot(spread_ref[...], jnp.concatenate(wide, axis=1), preferred_element_type=jnp.float32)
            for r in range(2):
                for o in range(n):
                    sums_ref[o, pl.ds(i * 2 + r, MAP_DEV, stride=deep), :] = out[
                        o * MAP_DEV : (o + 1) * MAP_DEV, r * LANES : (r + 1) * LANES
                    ]
            return carry

        lax.fori_loop(0, deep // 2, pair, 0)
        for o in range(n):
            sum_msg[q, o] = sums_ref[o].astype(jnp.bfloat16)
        got_sums[q, me] = sum_msg[q, me]
        for k in peers:
            sum_copy(q, partner(k), me).start()
        return carry

    lax.fori_loop(0, CHUNKS, reduce, 0)

    weights = [kern_ref[k].astype(jnp.bfloat16).astype(jnp.float32) for k in range(KW)]

    def finish(q, carry):
        for k in peers:
            sum_copy(q, partner(k), partner(k)).wait_recv()

        def place(s, carry):
            y = got_sums[q, s].astype(jnp.float32)
            for k in range(1, GROUPS):
                y = y + got_sums[q, s + k * near].astype(jnp.float32)
            out = weights[0] * y
            for k in range(1, KW):
                out = out + weights[k] * pltpu.roll(y, LANES - k, 1)
            at = pl.ds(pl.multiple_of((s * CHUNKS + q) * deep, deep), deep)
            for m in range(MAP_DEV):
                result_ref[m, at, :] = out[m * deep : (m + 1) * deep] * inv_ref[m : m + 1, :]
            return carry

        lax.fori_loop(0, near, place, 0)
        return carry

    lax.fori_loop(0, CHUNKS, finish, 0)

    for k in peers:
        fact_copy(partner(k), me).wait_send()
        for h in range(PHASES):
            cell_copy(h, partner(k), me).wait_send()
        for q in range(CHUNKS):
            sum_copy(q, partner(k), me).wait_send()
    for k in inner:
        for h in range(PHASES):
            for q in range(CHUNKS):
                row_copy(h, q, partner(k), me).wait_send()


def shards(n, radar_stack, filter_taps, filter_lengths, resample_kernel, tile_owner, map_slot, correlation, offsets):
    dates_here, rows, ranges = radar_stack.shape[1:]
    dates = n * dates_here
    tile_count = tile_owner.shape[0]
    near = n // GROUPS
    tiles = near * tile_count
    deep = 2 * dates // near // CHUNKS
    block = (PHASES, n, 2 * PATCH_AZ * dates_here, LANES)
    row_block = (PHASES, near, CHUNKS, deep * PATCH_AZ, LANES)
    sum_block = (CHUNKS, n, MAP_DEV * deep, LANES)
    facts = [x.reshape(1, tile_count) for x in (tile_owner, map_slot, offsets, correlation)]
    given = (filter_lengths, resample_kernel, radar_stack, filter_taps, *facts)

    dma = pltpu.SemaphoreType.DMA
    return pl.pallas_call(
        partial(flow_kernel, n),
        out_shape=jax.ShapeDtypeStruct((MAP_DEV, 2 * dates, TILE), jnp.float32),
        in_specs=[HBM] * len(given),
        out_specs=VMEM,
        scratch_shapes=[
            pltpu.VMEM(block, jnp.bfloat16),
            pltpu.VMEM(block, jnp.bfloat16),
            pltpu.VMEM((FACTS, tiles), jnp.float32),
            pltpu.VMEM((n, FACTS, tiles), jnp.float32),
            pltpu.VMEM(block[1:], jnp.float32),
            pltpu.VMEM((LANES // PATCH_RG, LANES, 2 * dates), jnp.bfloat16),
            pltpu.VMEM((PATCH_AZ, LANES, 2 * dates), jnp.bfloat16),
            pltpu.VMEM((2 * dates * PATCH_AZ, LANES), jnp.float32),
            pltpu.VMEM(row_block, jnp.bfloat16),
            pltpu.VMEM(row_block, jnp.bfloat16),
            pltpu.VMEM(sum_block[1:], jnp.float32),
            pltpu.VMEM(sum_block, jnp.bfloat16),
            pltpu.VMEM(sum_block, jnp.bfloat16),
            pltpu.VMEM((dates_here, 2 * rows, 2 * rows), jnp.bfloat16),
            pltpu.VMEM((n * MAP_DEV, tiles), jnp.bfloat16),
            pltpu.VMEM(((TILE - 1).bit_length(), tiles, LANES), jnp.int32),
            pltpu.VMEM((MAP_DEV, LANES), jnp.float32),
            pltpu.SMEM(filter_lengths.shape, jnp.int32),
            pltpu.SMEM(resample_kernel.shape, jnp.float32),
            pltpu.VMEM(radar_stack.shape, radar_stack.dtype),
            pltpu.VMEM(filter_taps.shape, jnp.float32),
            pltpu.VMEM((1, tile_count), jnp.int32),
            pltpu.VMEM((1, tile_count), jnp.int32),
            pltpu.VMEM((1, tile_count), jnp.int32),
            pltpu.VMEM((1, tile_count), jnp.int32),
            dma((PHASES,)),
            dma((n,)),
            dma((n,)),
            dma((PHASES, n)),
            dma((PHASES, n)),
            dma((PHASES, CHUNKS, near)),
            dma((PHASES, CHUNKS, near)),
            dma((CHUNKS, n)),
            dma((CHUNKS, n)),
            dma((len(given),)),
        ],
        compiler_params=pltpu.CompilerParams(collective_id=0, has_side_effects=True, vmem_limit_bytes=BIG),
        name="flow",
    )(*[pltpu.with_memory_space_constraint(x, pltpu.MemorySpace.HBM) for x in given])


def solution(mesh):
    in_specs = (
        P(None, "date", "grp", None),
        P(None, "date", None),
        P("date"),
        P(),
        P(("grp", "date"), None),
        P(("grp", "date")),
        P(("grp", "date")),
        P(("grp", "date")),
    )
    out_specs = P(("grp", "date"), None, None)
    return jax.shard_map(
        partial(shards, mesh.shape["date"]), mesh=mesh, in_specs=in_specs, out_specs=out_specs, check_vma=False
    )
```

```python
from functools import partial

import jax
import jax.numpy as jnp
from jax import lax
from jax.experimental import pallas as pl
from jax.experimental.pallas import tpu as pltpu
from jax.sharding import PartitionSpec as P

PATCH_AZ = 8
PATCH_RG = 16
TILE = 128
KW = 4
MAP_DEV = 8
LANES = 128
PHASES = 2
TOGETHER = 4
SWEEPS = 3
GROUPS = 2
CHUNKS = 4
FACTS = 8
PAIR = 2 * PATCH_AZ

diag_load = 0.5
small_eps = 1e-05
MESH = pl.DeviceIdType.MESH
VMEM = pl.BlockSpec(memory_space=pltpu.VMEM)
HBM = pl.BlockSpec(memory_space=pltpu.MemorySpace.HBM)
BIG = 32 * 1024 * 1024


def across(x, y):
    return lax.dot_general(x, y, (((0,), (0,)), ((), ())), preferred_element_type=jnp.float32)


def operator_of(top):
    dates = top.shape[0]
    return jnp.concatenate([top, jnp.concatenate([-top[:, dates:], top[:, :dates]], axis=1)], axis=0)


def whiten_windows(z_ref, first, white_ref, half_ref, cells_ref, left_ref, right_ref):
    looks, dates = z_ref.shape[1], z_ref.shape[2] // 2
    eye = lax.broadcasted_iota(jnp.int32, (dates, dates), 0) == lax.broadcasted_iota(jnp.int32, (dates, dates), 1)
    overs = []
    for q in range(TOGETHER):
        zt = z_ref[first + q]
        zt_re, zt_im = zt[:, :dates], zt[:, dates:]
        top = across(
            jnp.concatenate([zt_re, zt_im], axis=0),
            jnp.concatenate([zt, jnp.concatenate([zt_im, -zt_re], axis=1)], axis=0),
        )
        diagonal = jnp.where(eye, top[:, :dates], 0.0)
        scale_col = lax.rsqrt(jnp.sum(diagonal, axis=1, keepdims=True) * (1.0 / looks) + small_eps) * (1.0 / looks)
        scale_row = lax.rsqrt(jnp.sum(diagonal, axis=0, keepdims=True) * (1.0 / looks) + small_eps)
        outer = scale_col * scale_row
        coher_re = top[:, :dates] * outer + jnp.where(eye, diag_load, 0.0)
        coher_im = top[:, dates:] * outer
        sums = jnp.sum(jnp.abs(coher_re) + jnp.abs(coher_im), axis=0, keepdims=True)
        over = 1.0 / jnp.max(sums, axis=1, keepdims=True)
        half = jnp.concatenate([coher_re, coher_im], axis=1) * (0.5 * over)
        half_ref[q] = half
        rounded = half.astype(jnp.bfloat16)
        left_ref[q] = jnp.concatenate([rounded, zt], axis=0)
        right_ref[q] = operator_of(rounded)
        overs.append(over)
    for stage in range(SWEEPS - 1):
        for q in range(TOGETHER):
            both = jnp.dot(left_ref[q], right_ref[q], preferred_element_type=jnp.float32)
            half = half_ref[q] - both[:dates]
            if stage == 0:
                cells = z_ref[first + q].astype(jnp.float32) - both[dates:]
            else:
                cells = cells_ref[q] - both[dates:]
            rounded = half.astype(jnp.bfloat16)
            if stage < SWEEPS - 2:
                half_ref[q] = half
                left_ref[q, :dates] = rounded
            cells_ref[q] = cells
            left_ref[q, dates:] = cells.astype(jnp.bfloat16)
            right_ref[q] = operator_of(rounded * (2.0 ** (stage + 1)))
    for q in range(TOGETHER):
        applied = jnp.dot(left_ref[q, dates:], right_ref[q], preferred_element_type=jnp.float32)
        white = ((cells_ref[q] - applied) * (2.0**SWEEPS * overs[q])).astype(jnp.bfloat16)
        for a in range(PATCH_AZ):
            white_ref[a, pl.ds((first + q) * PATCH_RG, PATCH_RG), :] = white[a * PATCH_RG : (a + 1) * PATCH_RG]


def flow_kernel(n, *refs):
    inputs, refs = refs[:8], refs[8:]
    result_ref, cells_ref, got_cells, facts_ref, got_facts, cell_ref, z_ref, white_ref, flat_ref = refs[:9]
    row_msg, got_rows, sum_msg, got_sums, operator_ref, spread_ref, shift_ref, inv_ref = refs[9:17]
    work, local, refs = refs[17:21], refs[21:29], refs[29:]
    len_ref, kern_ref, radar_ref, taps_ref = local[:4]
    fact_refs = local[4:8]
    own_sem, fact_send, fact_recv, cell_send, cell_recv, row_send, row_recv, sum_send, sum_recv, load_sem = refs
    me = lax.axis_index("date")
    dates_here, rows = radar_ref.shape[1], radar_ref.shape[2]
    taps, tile_count = taps_ref.shape[2], fact_refs[0].shape[1]
    total = n * dates_here
    windows = LANES // PATCH_RG
    near = n // GROUPS
    group, rank = me // near, me % near
    slots = spread_ref.shape[1]
    deep = 2 * total // near // CHUNKS

    barrier = pltpu.get_barrier_semaphore()
    loads = [pltpu.make_async_copy(x, y, load_sem.at[i]) for i, (x, y) in enumerate(zip(inputs, local))]
    for load in loads:
        load.start()
    for k in range(1, n):
        pl.semaphore_signal(barrier, inc=1, device_id={"date": lax.rem(me + k, n)}, device_id_type=MESH)
    own = [pltpu.make_async_copy(cells_ref.at[h, me], got_cells.at[h, me], own_sem.at[h]) for h in range(PHASES)]

    def send(src, dst, send_sem, recv_sem, peer):
        pltpu.make_async_remote_copy(
            src_ref=src,
            dst_ref=dst,
            send_sem=send_sem,
            recv_sem=recv_sem,
            device_id={"date": peer},
            device_id_type=MESH,
        ).start()

    def drain(ref, sem):
        pltpu.make_async_copy(ref, ref, sem).wait()

    def partner(k):
        peer, bit = me, 1
        while bit < n:
            peer = peer + (k // bit) % 2 * (1 - (me // bit) % 2 * 2) * bit
            bit *= 2
        return peer

    def turn(i):
        return n - 1 - i // 2 - i % 2 * (n // 2)

    peers = [turn(i) for i in range(n - 1)]
    inner = list(range(near - 1, 0, -1))

    for load in loads:
        load.wait()
    position = lax.broadcasted_iota(jnp.int32, (1, taps), 1)
    a_iota = lax.broadcasted_iota(jnp.int32, (rows, rows), 0)
    b_iota = lax.broadcasted_iota(jnp.int32, (rows, rows), 1)
    tap_at = b_iota - a_iota + taps // 2
    inside = jnp.logical_and(tap_at >= 0, tap_at < taps)

    def toeplitz(d, which):
        kept = jnp.where(position < len_ref[d], taps_ref[which, pl.ds(d, 1), :], 0.0)
        rolled = pltpu.roll(jnp.broadcast_to(kept, (rows, taps)), taps // 2, 1, stride=1, stride_axis=0)
        return jnp.where(inside, jnp.concatenate([rolled] * (rows // taps), axis=1), 0.0)

    for h in range(PHASES):
        for d in range(dates_here):
            if h == 0:
                t_re, t_im = toeplitz(d, 0), toeplitz(d, 1)
                operator_ref[d] = jnp.concatenate(
                    [jnp.concatenate([t_re, -t_im], axis=1), jnp.concatenate([t_im, t_re], axis=1)], axis=0
                ).astype(jnp.bfloat16)
            side = slice(h * LANES, (h + 1) * LANES)
            columns = jnp.concatenate([radar_ref[0, d, :, side], radar_ref[1, d, :, side]], axis=0)
            product = jnp.dot(operator_ref[d], columns, preferred_element_type=jnp.float32)
            for p in range(n):
                for part in range(2):
                    top = part * rows + p * PATCH_AZ
                    cell_ref[p, pl.ds(part * PATCH_AZ * dates_here + d, PATCH_AZ, stride=dates_here), :] = product[
                        top : top + PATCH_AZ
                    ]
        for p in range(n):
            cells_ref[h, p] = cell_ref[p].astype(jnp.bfloat16)
        if h == 0:
            pl.semaphore_wait(barrier, n - 1)
        for k in peers:
            send(cells_ref.at[h, partner(k)], got_cells.at[h, me], cell_send.at[0], cell_recv.at[h], partner(k))
        own[h].start()

    tile_at = lax.broadcasted_iota(jnp.int32, (LANES, slots), 0)
    lane_at = lax.broadcasted_iota(jnp.int32, (LANES, slots), 1)
    placed = ((tile_at & 1) * near + rank) * PAIR + (tile_at >> 1)
    hit = jnp.logical_or(lane_at == placed, lane_at == placed + PATCH_AZ)
    moving = jnp.where(jnp.logical_and(hit, tile_at < tile_count), 1.0, 0.0).astype(jnp.bfloat16)
    listed = jnp.concatenate([fact[...] for fact in fact_refs], axis=0).astype(jnp.float32)
    listed = jnp.concatenate([listed, jnp.zeros((FACTS - len(fact_refs), tile_count), jnp.float32)], axis=0)
    listed = jnp.concatenate([listed, jnp.zeros((FACTS, LANES - tile_count), jnp.float32)], axis=1)
    facts_ref[...] = jnp.dot(listed.astype(jnp.bfloat16), moving, preferred_element_type=jnp.float32)
    for k in peers:
        send(facts_ref, got_facts.at[me], fact_send.at[0], fact_recv.at[0], partner(k))
    got_facts[me] = facts_ref[...]

    apart = lax.broadcasted_iota(jnp.int32, (TILE, TILE), 0) - lax.broadcasted_iota(jnp.int32, (TILE, TILE), 1) + TILE
    for t in range(tile_count):
        shift = fact_refs[2][:, t : t + 1]
        shift_ref[t] = jnp.where(((apart - shift) & (TILE - 1)) == 0, 1.0, 0.0).astype(jnp.bfloat16)

    drain(got_facts.at[pl.ds(0, n - 1)], fact_recv.at[0])
    here = got_facts[group * near]
    for s in range(1, near):
        here = here + got_facts[group * near + s]
    row_at = lax.broadcasted_iota(jnp.int32, spread_ref.shape, 0)
    slot_at = lax.broadcasted_iota(jnp.int32, spread_ref.shape, 1)
    named = ((row_at >> 4) * MAP_DEV + (row_at & 7)).astype(jnp.float32)
    same = jnp.logical_and(named == here[0:1] * MAP_DEV + here[1:2], ((row_at ^ slot_at) & PATCH_AZ) == 0)
    spread_ref[...] = jnp.where(same, here[3:4], 0.0).astype(jnp.bfloat16)
    mine = (me * MAP_DEV + lax.broadcasted_iota(jnp.int32, (MAP_DEV, slots), 0)).astype(jnp.float32)
    once = (lax.broadcasted_iota(jnp.int32, (MAP_DEV, slots), 1) & PATCH_AZ) == 0
    count = jnp.zeros((MAP_DEV, slots), jnp.float32)
    for k in range(GROUPS):
        facts = got_facts[k * near]
        for s in range(1, near):
            facts = facts + got_facts[k * near + s]
        owned = jnp.logical_and(mine == facts[0:1] * MAP_DEV + facts[1:2], once)
        count = count + jnp.where(owned, facts[3:4], 0.0)
    inv_ref[...] = jnp.broadcast_to(1.0 / jnp.maximum(jnp.sum(count, axis=1, keepdims=True), 1.0), inv_ref.shape)

    for h in range(PHASES):
        own[h].wait()
        drain(got_cells.at[h, pl.ds(0, n - 1)], cell_recv.at[h])
        for s in range(n):
            cell_ref[s] = got_cells[h, s].astype(jnp.float32)
        for part in range(2):
            for a in range(PATCH_AZ):
                at = pl.ds((part * PATCH_AZ + a) * dates_here, dates_here)
                line = jnp.concatenate([cell_ref[s, at, :] for s in range(n)], axis=0).T.astype(jnp.bfloat16)
                for j in range(windows):
                    z_ref[j, a * PATCH_RG : (a + 1) * PATCH_RG, part * total : (part + 1) * total] = line[
                        j * PATCH_RG : (j + 1) * PATCH_RG
                    ]

        def whiten(i, carry):
            whiten_windows(z_ref, i * TOGETHER, white_ref, *work)
            return carry

        lax.fori_loop(0, windows // TOGETHER, whiten, 0)

        for a in range(PATCH_AZ):
            flat_ref[pl.ds(a, 2 * total, stride=PATCH_AZ), :] = across(white_ref[a], shift_ref[a * 2 + h])
        for q in range(CHUNKS):
            for to in range(near):
                row_msg[h, to, q] = flat_ref[
                    pl.ds((to * CHUNKS + q) * deep * PATCH_AZ, deep * PATCH_AZ), :
                ].astype(jnp.bfloat16)
            got_rows[h, rank, q] = row_msg[h, rank, q]
            if h == PHASES - 1:
                for k in inner:
                    to = partner(k) % near
                    send(row_msg.at[h, to, q], got_rows.at[h, rank, q], row_send.at[0], row_recv.at[1 + q], partner(k))
        if h < PHASES - 1:
            for k in inner:
                to = partner(k) % near
                send(row_msg.at[h, to], got_rows.at[h, rank], row_send.at[0], row_recv.at[0], partner(k))

    drain(got_rows.at[0, pl.ds(0, near - 1)], row_recv.at[0])

    def reduce(q, carry):
        drain(got_rows.at[1, pl.ds(0, near - 1), q], row_recv.at[1 + q])
        for i in range(deep // 2):
            at = slice(i * PAIR, (i + 1) * PAIR)
            cells = jnp.concatenate([got_rows[h, s, q, at, :] for h in range(PHASES) for s in range(near)], axis=0)
            out = jnp.dot(spread_ref[...], cells, preferred_element_type=jnp.float32).astype(jnp.bfloat16)
            for o in range(n):
                sum_msg[q, o, at, :] = out[o * PAIR : (o + 1) * PAIR]
        got_sums[q, me] = sum_msg[q, me]
        for k in peers:
            send(sum_msg.at[q, partner(k)], got_sums.at[q, me], sum_send.at[0], sum_recv.at[q], partner(k))
        return carry

    lax.fori_loop(0, CHUNKS, reduce, 0)

    weights = [kern_ref[k].astype(jnp.bfloat16).astype(jnp.float32) for k in range(KW)]

    def finish(q, carry):
        drain(got_sums.at[q, pl.ds(0, n - 1)], sum_recv.at[q])

        def place(s, carry):
            y = got_sums[q, s].astype(jnp.float32)
            for k in range(1, GROUPS):
                y = y + got_sums[q, s + k * near].astype(jnp.float32)
            out = weights[0] * y
            for k in range(1, KW):
                out = out + weights[k] * pltpu.roll(y, LANES - k, 1)
            for r in range(deep):
                at = pl.ds((s * CHUNKS + q) * deep + r, MAP_DEV, stride=2 * total)
                result_ref[at, :] = out[r * MAP_DEV : (r + 1) * MAP_DEV] * inv_ref[...]
            return carry

        lax.fori_loop(0, near, place, 0)
        return carry

    lax.fori_loop(0, CHUNKS, finish, 0)

    drain(got_facts.at[pl.ds(0, n - 1)], fact_send.at[0])
    drain(cells_ref.at[:, pl.ds(0, n - 1)], cell_send.at[0])
    drain(row_msg.at[:, pl.ds(0, near - 1)], row_send.at[0])
    drain(sum_msg.at[:, pl.ds(0, n - 1)], sum_send.at[0])


def shards(n, radar_stack, filter_taps, filter_lengths, resample_kernel, tile_owner, map_slot, correlation, offsets):
    dates_here, rows, ranges = radar_stack.shape[1:]
    dates = n * dates_here
    tile_count = tile_owner.shape[0]
    near = n // GROUPS
    slots = PHASES * near * PAIR
    deep = 2 * dates // near // CHUNKS
    block = (PHASES, n, 2 * PATCH_AZ * dates_here, LANES)
    row_block = (PHASES, near, CHUNKS, deep * PATCH_AZ, LANES)
    sum_block = (CHUNKS, n, MAP_DEV * deep, LANES)
    facts = [x.reshape(1, tile_count) for x in (tile_owner, map_slot, offsets, correlation)]
    given = (filter_lengths, resample_kernel, radar_stack, filter_taps, *facts)

    dma = pltpu.SemaphoreType.DMA
    result = pl.pallas_call(
        partial(flow_kernel, n),
        out_shape=jax.ShapeDtypeStruct((MAP_DEV * 2 * dates, TILE), jnp.float32),
        in_specs=[HBM] * len(given),
        out_specs=VMEM,
        scratch_shapes=[
            pltpu.VMEM(block, jnp.bfloat16),
            pltpu.VMEM(block, jnp.bfloat16),
            pltpu.VMEM((FACTS, slots), jnp.float32),
            pltpu.VMEM((n, FACTS, slots), jnp.float32),
            pltpu.VMEM(block[1:], jnp.float32),
            pltpu.VMEM((LANES // PATCH_RG, LANES, 2 * dates), jnp.bfloat16),
            pltpu.VMEM((PATCH_AZ, LANES, 2 * dates), jnp.bfloat16),
            pltpu.VMEM((2 * dates * PATCH_AZ, LANES), jnp.float32),
            pltpu.VMEM(row_block, jnp.bfloat16),
            pltpu.VMEM(row_block, jnp.bfloat16),
            pltpu.VMEM(sum_block, jnp.bfloat16),
            pltpu.VMEM(sum_block, jnp.bfloat16),
            pltpu.VMEM((dates_here, 2 * rows, 2 * rows), jnp.bfloat16),
            pltpu.VMEM((n * PAIR, slots), jnp.bfloat16),
            pltpu.VMEM((tile_count, TILE, TILE), jnp.bfloat16),
            pltpu.VMEM((MAP_DEV, LANES), jnp.float32),
            pltpu.VMEM((TOGETHER, dates, 2 * dates), jnp.float32),
            pltpu.VMEM((TOGETHER, LANES, 2 * dates), jnp.float32),
            pltpu.VMEM((TOGETHER, dates + LANES, 2 * dates), jnp.bfloat16),
            pltpu.VMEM((TOGETHER, 2 * dates, 2 * dates), jnp.bfloat16),
            pltpu.SMEM(filter_lengths.shape, jnp.int32),
            pltpu.SMEM(resample_kernel.shape, jnp.float32),
            pltpu.VMEM(radar_stack.shape, radar_stack.dtype),
            pltpu.VMEM(filter_taps.shape, jnp.float32),
            pltpu.VMEM((1, tile_count), jnp.int32),
            pltpu.VMEM((1, tile_count), jnp.int32),
            pltpu.VMEM((1, tile_count), jnp.int32),
            pltpu.VMEM((1, tile_count), jnp.int32),
            dma((PHASES,)),
            dma((1,)),
            dma((1,)),
            dma((1,)),
            dma((PHASES,)),
            dma((1,)),
            dma((1 + CHUNKS,)),
            dma((1,)),
            dma((CHUNKS,)),
            dma((len(given),)),
        ],
        compiler_params=pltpu.CompilerParams(collective_id=0, has_side_effects=True, vmem_limit_bytes=BIG),
        name="flow",
    )(*[pltpu.with_memory_space_constraint(x, pltpu.MemorySpace.HBM) for x in given])
    return result.reshape(MAP_DEV, 2 * dates, TILE)


def solution(mesh):
    in_specs = (
        P(None, "date", "grp", None),
        P(None, "date", None),
        P("date"),
        P(),
        P(("grp", "date"), None),
        P(("grp", "date")),
        P(("grp", "date")),
        P(("grp", "date")),
    )
    out_specs = P(("grp", "date"), None, None)
    return jax.shard_map(
        partial(shards, mesh.shape["date"]), mesh=mesh, in_specs=in_specs, out_specs=out_specs, check_vma=False
    )
```

```python
from functools import partial

import jax
import jax.numpy as jnp
from jax import lax
from jax.experimental import pallas as pl
from jax.experimental.pallas import tpu as pltpu
from jax.sharding import PartitionSpec as P

PATCH_AZ = 8
PATCH_RG = 16
TILE = 128
KW = 4
MAP_DEV = 8
LANES = 128
PHASES = 2
TOGETHER = 4
SWEEPS = 3
GROUPS = 2
CHUNKS = 4
FACTS = 8
PAIR = 2 * PATCH_AZ

diag_load = 0.5
small_eps = 1e-05
MESH = pl.DeviceIdType.MESH
VMEM = pl.BlockSpec(memory_space=pltpu.VMEM)
HBM = pl.BlockSpec(memory_space=pltpu.MemorySpace.HBM)
BIG = 32 * 1024 * 1024


def across(x, y):
    return lax.dot_general(x, y, (((0,), (0,)), ((), ())), preferred_element_type=jnp.float32)


def operator_of(top):
    dates = top.shape[0]
    return jnp.concatenate([top, jnp.concatenate([-top[:, dates:], top[:, :dates]], axis=1)], axis=0)


def whiten_windows(z_ref, first, white_ref, half_ref, cells_ref, left_ref, right_ref):
    looks, dates = z_ref.shape[1], z_ref.shape[2] // 2
    eye = lax.broadcasted_iota(jnp.int32, (dates, dates), 0) == lax.broadcasted_iota(jnp.int32, (dates, dates), 1)
    overs = []
    for q in range(TOGETHER):
        zt = z_ref[first + q]
        zt_re, zt_im = zt[:, :dates], zt[:, dates:]
        top = across(
            jnp.concatenate([zt_re, zt_im], axis=0),
            jnp.concatenate([zt, jnp.concatenate([zt_im, -zt_re], axis=1)], axis=0),
        )
        diagonal = jnp.where(eye, top[:, :dates], 0.0)
        scale_col = lax.rsqrt(jnp.sum(diagonal, axis=1, keepdims=True) * (1.0 / looks) + small_eps) * (1.0 / looks)
        scale_row = lax.rsqrt(jnp.sum(diagonal, axis=0, keepdims=True) * (1.0 / looks) + small_eps)
        outer = scale_col * scale_row
        coher_re = top[:, :dates] * outer + jnp.where(eye, diag_load, 0.0)
        coher_im = top[:, dates:] * outer
        sums = jnp.sum(jnp.abs(coher_re) + jnp.abs(coher_im), axis=0, keepdims=True)
        over = 1.0 / jnp.max(sums, axis=1, keepdims=True)
        half = jnp.concatenate([coher_re, coher_im], axis=1) * (0.5 * over)
        half_ref[q] = half
        rounded = half.astype(jnp.bfloat16)
        left_ref[q] = jnp.concatenate([rounded, zt], axis=0)
        right_ref[q] = operator_of(rounded)
        overs.append(over)
    for stage in range(SWEEPS - 1):
        for q in range(TOGETHER):
            both = jnp.dot(left_ref[q], right_ref[q], preferred_element_type=jnp.float32)
            half = half_ref[q] - both[:dates]
            if stage == 0:
                cells = z_ref[first + q].astype(jnp.float32) - both[dates:]
            else:
                cells = cells_ref[q] - both[dates:]
            rounded = half.astype(jnp.bfloat16)
            if stage < SWEEPS - 2:
                half_ref[q] = half
                left_ref[q, :dates] = rounded
            cells_ref[q] = cells
            left_ref[q, dates:] = cells.astype(jnp.bfloat16)
            right_ref[q] = operator_of(rounded * (2.0 ** (stage + 1)))
    for q in range(TOGETHER):
        applied = jnp.dot(left_ref[q, dates:], right_ref[q], preferred_element_type=jnp.float32)
        white = ((cells_ref[q] - applied) * (2.0**SWEEPS * overs[q])).astype(jnp.bfloat16)
        for a in range(PATCH_AZ):
            white_ref[a, pl.ds((first + q) * PATCH_RG, PATCH_RG), :] = white[a * PATCH_RG : (a + 1) * PATCH_RG]


def flow_kernel(n, *refs):
    inputs, refs = refs[:8], refs[8:]
    result_ref, cells_ref, got_cells, facts_ref, got_facts, cell_ref, z_ref, white_ref, flat_ref = refs[:9]
    row_msg, got_rows, sum_msg, got_sums, operator_ref, spread_ref, shift_ref, inv_ref = refs[9:17]
    work, local, refs = refs[17:21], refs[21:29], refs[29:]
    len_ref, kern_ref, radar_ref, taps_ref = local[:4]
    fact_refs = local[4:8]
    own_sem, fact_send, fact_recv, cell_send, cell_recv, row_send, row_recv, sum_send, sum_recv, load_sem = refs
    me = lax.axis_index("date")
    dates_here, rows = radar_ref.shape[1], radar_ref.shape[2]
    taps, tile_count = taps_ref.shape[2], fact_refs[0].shape[1]
    total = n * dates_here
    windows = LANES // PATCH_RG
    near = n // GROUPS
    group, rank = me // near, me % near
    slots = spread_ref.shape[1]
    deep = 2 * total // near // CHUNKS

    barrier = pltpu.get_barrier_semaphore()
    loads = [pltpu.make_async_copy(x, y, load_sem.at[i]) for i, (x, y) in enumerate(zip(inputs, local))]
    for load in loads:
        load.start()
    for k in range(1, n):
        pl.semaphore_signal(barrier, inc=1, device_id={"date": lax.rem(me + k, n)}, device_id_type=MESH)
    own = [pltpu.make_async_copy(cells_ref.at[h, me], got_cells.at[h, me], own_sem.at[h]) for h in range(PHASES)]

    def send(src, dst, send_sem, recv_sem, peer):
        pltpu.make_async_remote_copy(
            src_ref=src,
            dst_ref=dst,
            send_sem=send_sem,
            recv_sem=recv_sem,
            device_id={"date": peer},
            device_id_type=MESH,
        ).start()

    def drain(ref, sem):
        pltpu.make_async_copy(ref, ref, sem).wait()

    def partner(k):
        peer, bit = me, 1
        while bit < n:
            peer = peer + (k // bit) % 2 * (1 - (me // bit) % 2 * 2) * bit
            bit *= 2
        return peer

    def turn(i):
        return n - 1 - i // 2 - i % 2 * (n // 2)

    peers = [turn(i) for i in range(n - 1)]
    inner = list(range(near - 1, 0, -1))

    for load in loads:
        load.wait()
    tile_at = lax.broadcasted_iota(jnp.int32, (LANES, slots), 0)
    lane_at = lax.broadcasted_iota(jnp.int32, (LANES, slots), 1)
    placed = ((tile_at & 1) * near + rank) * PAIR + (tile_at >> 1)
    hit = jnp.logical_or(lane_at == placed, lane_at == placed + PATCH_AZ)
    moving = jnp.where(jnp.logical_and(hit, tile_at < tile_count), 1.0, 0.0).astype(jnp.bfloat16)
    listed = jnp.concatenate([fact[...] for fact in fact_refs], axis=0).astype(jnp.float32)
    listed = jnp.concatenate([listed, jnp.zeros((FACTS - len(fact_refs), tile_count), jnp.float32)], axis=0)
    listed = jnp.concatenate([listed, jnp.zeros((FACTS, LANES - tile_count), jnp.float32)], axis=1)
    facts_ref[...] = jnp.dot(listed.astype(jnp.bfloat16), moving, preferred_element_type=jnp.float32)
    position = lax.broadcasted_iota(jnp.int32, (1, taps), 1)
    a_iota = lax.broadcasted_iota(jnp.int32, (rows, rows), 0)
    b_iota = lax.broadcasted_iota(jnp.int32, (rows, rows), 1)
    tap_at = b_iota - a_iota + taps // 2
    inside = jnp.logical_and(tap_at >= 0, tap_at < taps)

    def toeplitz(d, which):
        kept = jnp.where(position < len_ref[d], taps_ref[which, pl.ds(d, 1), :], 0.0)
        rolled = pltpu.roll(jnp.broadcast_to(kept, (rows, taps)), taps // 2, 1, stride=1, stride_axis=0)
        return jnp.where(inside, jnp.concatenate([rolled] * (rows // taps), axis=1), 0.0)

    for h in range(PHASES):
        for d in range(dates_here):
            if h == 0:
                t_re, t_im = toeplitz(d, 0), toeplitz(d, 1)
                operator_ref[d] = jnp.concatenate(
                    [jnp.concatenate([t_re, -t_im], axis=1), jnp.concatenate([t_im, t_re], axis=1)], axis=0
                ).astype(jnp.bfloat16)
            side = slice(h * LANES, (h + 1) * LANES)
            columns = jnp.concatenate([radar_ref[0, d, :, side], radar_ref[1, d, :, side]], axis=0)
            product = jnp.dot(operator_ref[d], columns, preferred_element_type=jnp.float32)
            for p in range(n):
                for part in range(2):
                    top = part * rows + p * PATCH_AZ
                    cell_ref[p, pl.ds(part * PATCH_AZ * dates_here + d, PATCH_AZ, stride=dates_here), :] = product[
                        top : top + PATCH_AZ
                    ]
        for p in range(n):
            cells_ref[h, p] = cell_ref[p].astype(jnp.bfloat16)
        if h == 0:
            pl.semaphore_wait(barrier, n - 1)
            for k in peers:
                send(facts_ref, got_facts.at[me], fact_send.at[0], fact_recv.at[0], partner(k))
            got_facts[me] = facts_ref[...]
        for k in peers:
            send(cells_ref.at[h, partner(k)], got_cells.at[h, me], cell_send.at[0], cell_recv.at[h], partner(k))
        own[h].start()

    apart = lax.broadcasted_iota(jnp.int32, (TILE, TILE), 0) - lax.broadcasted_iota(jnp.int32, (TILE, TILE), 1) + TILE
    for t in range(tile_count):
        shift = fact_refs[2][:, t : t + 1]
        shift_ref[t] = jnp.where(((apart - shift) & (TILE - 1)) == 0, 1.0, 0.0).astype(jnp.bfloat16)

    def settle():
        drain(got_facts.at[pl.ds(0, n - 1)], fact_recv.at[0])
        here = got_facts[group * near]
        for s in range(1, near):
            here = here + got_facts[group * near + s]
        row_at = lax.broadcasted_iota(jnp.int32, spread_ref.shape, 0)
        slot_at = lax.broadcasted_iota(jnp.int32, spread_ref.shape, 1)
        named = ((row_at >> 4) * MAP_DEV + (row_at & 7)).astype(jnp.float32)
        same = jnp.logical_and(named == here[0:1] * MAP_DEV + here[1:2], ((row_at ^ slot_at) & PATCH_AZ) == 0)
        spread_ref[...] = jnp.where(same, here[3:4], 0.0).astype(jnp.bfloat16)
        mine = (me * MAP_DEV + lax.broadcasted_iota(jnp.int32, (MAP_DEV, slots), 0)).astype(jnp.float32)
        once = (lax.broadcasted_iota(jnp.int32, (MAP_DEV, slots), 1) & PATCH_AZ) == 0
        count = jnp.zeros((MAP_DEV, slots), jnp.float32)
        for k in range(GROUPS):
            facts = got_facts[k * near]
            for s in range(1, near):
                facts = facts + got_facts[k * near + s]
            owned = jnp.logical_and(mine == facts[0:1] * MAP_DEV + facts[1:2], once)
            count = count + jnp.where(owned, facts[3:4], 0.0)
        inv_ref[...] = jnp.broadcast_to(1.0 / jnp.maximum(jnp.sum(count, axis=1, keepdims=True), 1.0), inv_ref.shape)

    for h in range(PHASES):
        own[h].wait()
        drain(got_cells.at[h, pl.ds(0, n - 1)], cell_recv.at[h])
        for s in range(n):
            cell_ref[s] = got_cells[h, s].astype(jnp.float32)
        for part in range(2):
            for a in range(PATCH_AZ):
                at = pl.ds((part * PATCH_AZ + a) * dates_here, dates_here)
                line = jnp.concatenate([cell_ref[s, at, :] for s in range(n)], axis=0).T.astype(jnp.bfloat16)
                for j in range(windows):
                    z_ref[j, a * PATCH_RG : (a + 1) * PATCH_RG, part * total : (part + 1) * total] = line[
                        j * PATCH_RG : (j + 1) * PATCH_RG
                    ]

        def whiten(i, carry):
            whiten_windows(z_ref, i * TOGETHER, white_ref, *work)
            return carry

        lax.fori_loop(0, windows // TOGETHER, whiten, 0)

        for a in range(PATCH_AZ):
            flat_ref[pl.ds(a, 2 * total, stride=PATCH_AZ), :] = across(white_ref[a], shift_ref[a * 2 + h])
        for q in range(CHUNKS):
            for to in range(near):
                row_msg[h, to, q] = flat_ref[
                    pl.ds((to * CHUNKS + q) * deep * PATCH_AZ, deep * PATCH_AZ), :
                ].astype(jnp.bfloat16)
            got_rows[h, rank, q] = row_msg[h, rank, q]
            if h == PHASES - 1:
                for k in inner:
                    to = partner(k) % near
                    send(row_msg.at[h, to, q], got_rows.at[h, rank, q], row_send.at[0], row_recv.at[1 + q], partner(k))
        if h < PHASES - 1:
            for k in inner:
                to = partner(k) % near
                send(row_msg.at[h, to], got_rows.at[h, rank], row_send.at[0], row_recv.at[0], partner(k))
            settle()

    drain(got_rows.at[0, pl.ds(0, near - 1)], row_recv.at[0])

    def reduce(q, carry):
        drain(got_rows.at[1, pl.ds(0, near - 1), q], row_recv.at[1 + q])
        for i in range(deep // 2):
            at = slice(i * PAIR, (i + 1) * PAIR)
            cells = jnp.concatenate([got_rows[h, s, q, at, :] for h in range(PHASES) for s in range(near)], axis=0)
            out = jnp.dot(spread_ref[...], cells, preferred_element_type=jnp.float32).astype(jnp.bfloat16)
            for o in range(n):
                sum_msg[q, o, at, :] = out[o * PAIR : (o + 1) * PAIR]
        got_sums[q, me] = sum_msg[q, me]
        for k in peers:
            send(sum_msg.at[q, partner(k)], got_sums.at[q, me], sum_send.at[0], sum_recv.at[q], partner(k))
        return carry

    lax.fori_loop(0, CHUNKS, reduce, 0)

    weights = [kern_ref[k].astype(jnp.bfloat16).astype(jnp.float32) for k in range(KW)]

    def finish(q, carry):
        drain(got_sums.at[q, pl.ds(0, n - 1)], sum_recv.at[q])

        def place(s, carry):
            y = got_sums[q, s].astype(jnp.float32)
            for k in range(1, GROUPS):
                y = y + got_sums[q, s + k * near].astype(jnp.float32)
            out = weights[0] * y
            for k in range(1, KW):
                out = out + weights[k] * pltpu.roll(y, LANES - k, 1)
            for r in range(deep):
                at = pl.ds((s * CHUNKS + q) * deep + r, MAP_DEV, stride=2 * total)
                result_ref[at, :] = out[r * MAP_DEV : (r + 1) * MAP_DEV] * inv_ref[...]
            return carry

        lax.fori_loop(0, near, place, 0)
        return carry

    lax.fori_loop(0, CHUNKS, finish, 0)

    drain(got_facts.at[pl.ds(0, n - 1)], fact_send.at[0])
    drain(cells_ref.at[:, pl.ds(0, n - 1)], cell_send.at[0])
    drain(row_msg.at[:, pl.ds(0, near - 1)], row_send.at[0])
    drain(sum_msg.at[:, pl.ds(0, n - 1)], sum_send.at[0])


def shards(n, radar_stack, filter_taps, filter_lengths, resample_kernel, tile_owner, map_slot, correlation, offsets):
    dates_here, rows, ranges = radar_stack.shape[1:]
    dates = n * dates_here
    tile_count = tile_owner.shape[0]
    near = n // GROUPS
    slots = PHASES * near * PAIR
    deep = 2 * dates // near // CHUNKS
    block = (PHASES, n, 2 * PATCH_AZ * dates_here, LANES)
    row_block = (PHASES, near, CHUNKS, deep * PATCH_AZ, LANES)
    sum_block = (CHUNKS, n, MAP_DEV * deep, LANES)
    facts = [x.reshape(1, tile_count) for x in (tile_owner, map_slot, offsets, correlation)]
    given = (filter_lengths, resample_kernel, radar_stack, filter_taps, *facts)

    dma = pltpu.SemaphoreType.DMA
    result = pl.pallas_call(
        partial(flow_kernel, n),
        out_shape=jax.ShapeDtypeStruct((MAP_DEV * 2 * dates, TILE), jnp.float32),
        in_specs=[HBM] * len(given),
        out_specs=VMEM,
        scratch_shapes=[
            pltpu.VMEM(block, jnp.bfloat16),
            pltpu.VMEM(block, jnp.bfloat16),
            pltpu.VMEM((FACTS, slots), jnp.float32),
            pltpu.VMEM((n, FACTS, slots), jnp.float32),
            pltpu.VMEM(block[1:], jnp.float32),
            pltpu.VMEM((LANES // PATCH_RG, LANES, 2 * dates), jnp.bfloat16),
            pltpu.VMEM((PATCH_AZ, LANES, 2 * dates), jnp.bfloat16),
            pltpu.VMEM((2 * dates * PATCH_AZ, LANES), jnp.float32),
            pltpu.VMEM(row_block, jnp.bfloat16),
            pltpu.VMEM(row_block, jnp.bfloat16),
            pltpu.VMEM(sum_block, jnp.bfloat16),
            pltpu.VMEM(sum_block, jnp.bfloat16),
            pltpu.VMEM((dates_here, 2 * rows, 2 * rows), jnp.bfloat16),
            pltpu.VMEM((n * PAIR, slots), jnp.bfloat16),
            pltpu.VMEM((tile_count, TILE, TILE), jnp.bfloat16),
            pltpu.VMEM((MAP_DEV, LANES), jnp.float32),
            pltpu.VMEM((TOGETHER, dates, 2 * dates), jnp.float32),
            pltpu.VMEM((TOGETHER, LANES, 2 * dates), jnp.float32),
            pltpu.VMEM((TOGETHER, dates + LANES, 2 * dates), jnp.bfloat16),
            pltpu.VMEM((TOGETHER, 2 * dates, 2 * dates), jnp.bfloat16),
            pltpu.SMEM(filter_lengths.shape, jnp.int32),
            pltpu.SMEM(resample_kernel.shape, jnp.float32),
            pltpu.VMEM(radar_stack.shape, radar_stack.dtype),
            pltpu.VMEM(filter_taps.shape, jnp.float32),
            pltpu.VMEM((1, tile_count), jnp.int32),
            pltpu.VMEM((1, tile_count), jnp.int32),
            pltpu.VMEM((1, tile_count), jnp.int32),
            pltpu.VMEM((1, tile_count), jnp.int32),
            dma((PHASES,)),
            dma((1,)),
            dma((1,)),
            dma((1,)),
            dma((PHASES,)),
            dma((1,)),
            dma((1 + CHUNKS,)),
            dma((1,)),
            dma((CHUNKS,)),
            dma((len(given),)),
        ],
        compiler_params=pltpu.CompilerParams(collective_id=0, has_side_effects=True, vmem_limit_bytes=BIG),
        name="flow",
    )(*[pltpu.with_memory_space_constraint(x, pltpu.MemorySpace.HBM) for x in given])
    return result.reshape(MAP_DEV, 2 * dates, TILE)


def solution(mesh):
    in_specs = (
        P(None, "date", "grp", None),
        P(None, "date", None),
        P("date"),
        P(),
        P(("grp", "date"), None),
        P(("grp", "date")),
        P(("grp", "date")),
        P(("grp", "date")),
    )
    out_specs = P(("grp", "date"), None, None)
    return jax.shard_map(
        partial(shards, mesh.shape["date"]), mesh=mesh, in_specs=in_specs, out_specs=out_specs, check_vma=False
    )
```

```python
from functools import partial

import jax
import jax.numpy as jnp
from jax import lax
from jax.experimental import pallas as pl
from jax.experimental.pallas import tpu as pltpu
from jax.sharding import PartitionSpec as P

PATCH_AZ = 8
PATCH_RG = 16
TILE = 128
KW = 4
MAP_DEV = 8
LANES = 128
PHASES = 2
TOGETHER = 4
SWEEPS = 3
GROUPS = 2
CHUNKS = 8
FACTS = 8
PAIR = 2 * PATCH_AZ

diag_load = 0.5
small_eps = 1e-05
MESH = pl.DeviceIdType.MESH
VMEM = pl.BlockSpec(memory_space=pltpu.VMEM)
HBM = pl.BlockSpec(memory_space=pltpu.MemorySpace.HBM)
BIG = 32 * 1024 * 1024


def across(x, y):
    return lax.dot_general(x, y, (((0,), (0,)), ((), ())), preferred_element_type=jnp.float32)


def operator_of(top):
    dates = top.shape[0]
    return jnp.concatenate([top, jnp.concatenate([-top[:, dates:], top[:, :dates]], axis=1)], axis=0)


def whiten_windows(z_ref, first, white_ref, half_ref, cells_ref, left_ref, right_ref):
    looks, dates = z_ref.shape[1], z_ref.shape[2] // 2
    eye = lax.broadcasted_iota(jnp.int32, (dates, dates), 0) == lax.broadcasted_iota(jnp.int32, (dates, dates), 1)
    overs = []
    for q in range(TOGETHER):
        zt = z_ref[first + q]
        zt_re, zt_im = zt[:, :dates], zt[:, dates:]
        top = across(
            jnp.concatenate([zt_re, zt_im], axis=0),
            jnp.concatenate([zt, jnp.concatenate([zt_im, -zt_re], axis=1)], axis=0),
        )
        diagonal = jnp.where(eye, top[:, :dates], 0.0)
        scale_col = lax.rsqrt(jnp.sum(diagonal, axis=1, keepdims=True) * (1.0 / looks) + small_eps) * (1.0 / looks)
        scale_row = lax.rsqrt(jnp.sum(diagonal, axis=0, keepdims=True) * (1.0 / looks) + small_eps)
        outer = scale_col * scale_row
        coher_re = top[:, :dates] * outer + jnp.where(eye, diag_load, 0.0)
        coher_im = top[:, dates:] * outer
        sums = jnp.sum(jnp.abs(coher_re) + jnp.abs(coher_im), axis=0, keepdims=True)
        over = 1.0 / jnp.max(sums, axis=1, keepdims=True)
        half = jnp.concatenate([coher_re, coher_im], axis=1) * (0.5 * over)
        half_ref[q] = half
        rounded = half.astype(jnp.bfloat16)
        left_ref[q] = jnp.concatenate([rounded, zt], axis=0)
        right_ref[q] = operator_of(rounded)
        overs.append(over)
    for stage in range(SWEEPS - 1):
        for q in range(TOGETHER):
            both = jnp.dot(left_ref[q], right_ref[q], preferred_element_type=jnp.float32)
            half = half_ref[q] - both[:dates]
            if stage == 0:
                cells = z_ref[first + q].astype(jnp.float32) - both[dates:]
            else:
                cells = cells_ref[q] - both[dates:]
            rounded = half.astype(jnp.bfloat16)
            if stage < SWEEPS - 2:
                half_ref[q] = half
                left_ref[q, :dates] = rounded
            cells_ref[q] = cells
            left_ref[q, dates:] = cells.astype(jnp.bfloat16)
            right_ref[q] = operator_of(rounded * (2.0 ** (stage + 1)))
    for q in range(TOGETHER):
        applied = jnp.dot(left_ref[q, dates:], right_ref[q], preferred_element_type=jnp.float32)
        white = ((cells_ref[q] - applied) * (2.0**SWEEPS * overs[q])).astype(jnp.bfloat16)
        for a in range(PATCH_AZ):
            white_ref[a, pl.ds((first + q) * PATCH_RG, PATCH_RG), :] = white[a * PATCH_RG : (a + 1) * PATCH_RG]


def flow_kernel(n, *refs):
    inputs, refs = refs[:8], refs[8:]
    result_ref, cells_ref, got_cells, split_ref, got_split, facts_ref, got_facts, cell_ref, z_ref, white_ref, flat_ref = refs[:11]
    row_msg, got_rows, sum_msg, got_sums, operator_ref, spread_ref, shift_ref, inv_ref = refs[11:19]
    work, local, refs = refs[19:23], refs[23:31], refs[31:]
    len_ref, kern_ref, radar_ref, taps_ref = local[:4]
    fact_refs = local[4:8]
    own_sem, fact_send, fact_recv, cell_send, cell_recv, row_send, row_recv, sum_send, sum_recv, load_sem = refs
    me = lax.axis_index("date")
    dates_here, rows = radar_ref.shape[1], radar_ref.shape[2]
    taps, tile_count = taps_ref.shape[2], fact_refs[0].shape[1]
    total = n * dates_here
    windows = LANES // PATCH_RG
    near = n // GROUPS
    group, rank = me // near, me % near
    slots = spread_ref.shape[1]
    deep = 2 * total // near // CHUNKS

    barrier = pltpu.get_barrier_semaphore()
    loads = [pltpu.make_async_copy(x, y, load_sem.at[i]) for i, (x, y) in enumerate(zip(inputs, local))]
    for load in loads:
        load.start()
    for k in range(1, n):
        pl.semaphore_signal(barrier, inc=1, device_id={"date": lax.rem(me + k, n)}, device_id_type=MESH)
    own = [pltpu.make_async_copy(cells_ref.at[me], got_cells.at[me], own_sem.at[0])]
    own += [pltpu.make_async_copy(split_ref.at[u, me], got_split.at[u, me], own_sem.at[1 + u]) for u in range(2)]

    def send(src, dst, send_sem, recv_sem, peer):
        pltpu.make_async_remote_copy(
            src_ref=src,
            dst_ref=dst,
            send_sem=send_sem,
            recv_sem=recv_sem,
            device_id={"date": peer},
            device_id_type=MESH,
        ).start()

    def drain(ref, sem):
        pltpu.make_async_copy(ref, ref, sem).wait()

    def partner(k):
        peer, bit = me, 1
        while bit < n:
            peer = peer + (k // bit) % 2 * (1 - (me // bit) % 2 * 2) * bit
            bit *= 2
        return peer

    def turn(i):
        return n - 1 - i // 2 - i % 2 * (n // 2)

    peers = [turn(i) for i in range(n - 1)]
    inner = list(range(near - 1, 0, -1))

    for load in loads:
        load.wait()
    tile_at = lax.broadcasted_iota(jnp.int32, (LANES, slots), 0)
    lane_at = lax.broadcasted_iota(jnp.int32, (LANES, slots), 1)
    placed = ((tile_at & 1) * near + rank) * PAIR + (tile_at >> 1)
    hit = jnp.logical_or(lane_at == placed, lane_at == placed + PATCH_AZ)
    moving = jnp.where(jnp.logical_and(hit, tile_at < tile_count), 1.0, 0.0).astype(jnp.bfloat16)
    listed = jnp.concatenate([fact[...] for fact in fact_refs], axis=0).astype(jnp.float32)
    listed = jnp.concatenate([listed, jnp.zeros((FACTS - len(fact_refs), tile_count), jnp.float32)], axis=0)
    listed = jnp.concatenate([listed, jnp.zeros((FACTS, LANES - tile_count), jnp.float32)], axis=1)
    facts_ref[...] = jnp.dot(listed.astype(jnp.bfloat16), moving, preferred_element_type=jnp.float32)
    position = lax.broadcasted_iota(jnp.int32, (1, taps), 1)
    a_iota = lax.broadcasted_iota(jnp.int32, (rows, rows), 0)
    b_iota = lax.broadcasted_iota(jnp.int32, (rows, rows), 1)
    tap_at = b_iota - a_iota + taps // 2
    inside = jnp.logical_and(tap_at >= 0, tap_at < taps)

    def toeplitz(d, which):
        kept = jnp.where(position < len_ref[d], taps_ref[which, pl.ds(d, 1), :], 0.0)
        rolled = pltpu.roll(jnp.broadcast_to(kept, (rows, taps)), taps // 2, 1, stride=1, stride_axis=0)
        return jnp.where(inside, jnp.concatenate([rolled] * (rows // taps), axis=1), 0.0)

    for h in range(PHASES):
        for d in range(dates_here):
            if h == 0:
                t_re, t_im = toeplitz(d, 0), toeplitz(d, 1)
                operator_ref[d] = jnp.concatenate(
                    [jnp.concatenate([t_re, -t_im], axis=1), jnp.concatenate([t_im, t_re], axis=1)], axis=0
                ).astype(jnp.bfloat16)
            side = slice(h * LANES, (h + 1) * LANES)
            columns = jnp.concatenate([radar_ref[0, d, :, side], radar_ref[1, d, :, side]], axis=0)
            product = jnp.dot(operator_ref[d], columns, preferred_element_type=jnp.float32)
            for p in range(n):
                for part in range(2):
                    top = part * rows + p * PATCH_AZ
                    cell_ref[p, pl.ds(part * PATCH_AZ * dates_here + d, PATCH_AZ, stride=dates_here), :] = product[
                        top : top + PATCH_AZ
                    ]
        if h == 0:
            for p in range(n):
                cells_ref[p] = cell_ref[p].astype(jnp.bfloat16)
            pl.semaphore_wait(barrier, n - 1)
            for k in peers:
                send(facts_ref, got_facts.at[me], fact_send.at[0], fact_recv.at[0], partner(k))
            got_facts[me] = facts_ref[...]
            for k in peers:
                send(cells_ref.at[partner(k)], got_cells.at[me], cell_send.at[0], cell_recv.at[0], partner(k))
            own[0].start()
        else:
            low = lax.broadcasted_iota(jnp.int32, (PATCH_AZ * dates_here, LANES), 1) < LANES // 2
            for p in range(n):
                lines = cell_ref[p].reshape(PATCH_AZ, 2, dates_here, LANES)
                even, odd = [lines[:, i].reshape(PATCH_AZ * dates_here, LANES) for i in range(2)]
                split_ref[0, p] = jnp.where(low, even, pltpu.roll(odd, LANES // 2, 1)).astype(jnp.bfloat16)
                split_ref[1, p] = jnp.where(low, pltpu.roll(even, LANES // 2, 1), odd).astype(jnp.bfloat16)
            for u in range(2):
                for k in peers:
                    send(
                        split_ref.at[u, partner(k)], got_split.at[u, me], cell_send.at[1], cell_recv.at[1 + u], partner(k)
                    )
                own[1 + u].start()

    apart = lax.broadcasted_iota(jnp.int32, (TILE, TILE), 0) - lax.broadcasted_iota(jnp.int32, (TILE, TILE), 1) + TILE
    for t in range(tile_count):
        shift = fact_refs[2][:, t : t + 1]
        step = (apart - shift) & (TILE - 1)
        circ = jnp.zeros((TILE, TILE), jnp.float32)
        for k in range(KW):
            circ = jnp.where(step == k, kern_ref[k], circ)
        shift_ref[t] = circ.astype(jnp.bfloat16)

    def settle():
        drain(got_facts.at[pl.ds(0, n - 1)], fact_recv.at[0])
        here = got_facts[group * near]
        for s in range(1, near):
            here = here + got_facts[group * near + s]
        row_at = lax.broadcasted_iota(jnp.int32, spread_ref.shape, 0)
        slot_at = lax.broadcasted_iota(jnp.int32, spread_ref.shape, 1)
        named = ((row_at >> 4) * MAP_DEV + (row_at & 7)).astype(jnp.float32)
        same = jnp.logical_and(named == here[0:1] * MAP_DEV + here[1:2], ((row_at ^ slot_at) & PATCH_AZ) == 0)
        spread_ref[...] = jnp.where(same, here[3:4], 0.0).astype(jnp.bfloat16)
        mine = (me * MAP_DEV + lax.broadcasted_iota(jnp.int32, (MAP_DEV, slots), 0)).astype(jnp.float32)
        once = (lax.broadcasted_iota(jnp.int32, (MAP_DEV, slots), 1) & PATCH_AZ) == 0
        count = jnp.zeros((MAP_DEV, slots), jnp.float32)
        for k in range(GROUPS):
            facts = got_facts[k * near]
            for s in range(1, near):
                facts = facts + got_facts[k * near + s]
            owned = jnp.logical_and(mine == facts[0:1] * MAP_DEV + facts[1:2], once)
            count = count + jnp.where(owned, facts[3:4], 0.0)
        inv_ref[...] = jnp.broadcast_to(1.0 / jnp.maximum(jnp.sum(count, axis=1, keepdims=True), 1.0), inv_ref.shape)

    def whiten(i, carry):
        whiten_windows(z_ref, i * TOGETHER, white_ref, *work)
        return carry

    def line_of(at):
        return jnp.concatenate([cell_ref[s, at, :] for s in range(n)], axis=0).T.astype(jnp.bfloat16)

    for h in range(PHASES):
        if h == 0:
            own[0].wait()
            drain(got_cells.at[pl.ds(0, n - 1)], cell_recv.at[0])
            for s in range(n):
                cell_ref[s] = got_cells[s].astype(jnp.float32)
            for part in range(2):
                for a in range(PATCH_AZ):
                    line = line_of(pl.ds((part * PATCH_AZ + a) * dates_here, dates_here))
                    for j in range(windows):
                        z_ref[j, a * PATCH_RG : (a + 1) * PATCH_RG, part * total : (part + 1) * total] = line[
                            j * PATCH_RG : (j + 1) * PATCH_RG
                        ]
            lax.fori_loop(0, windows // TOGETHER, whiten, 0)
        else:
            for u in range(2):
                own[1 + u].wait()
                drain(got_split.at[u, pl.ds(0, n - 1)], cell_recv.at[1 + u])
                for s in range(n):
                    cell_ref[s, : PATCH_AZ * dates_here] = got_split[u, s].astype(jnp.float32)
                for part in range(2):
                    for b in range(PATCH_AZ // 2):
                        line = line_of(pl.ds((part * (PATCH_AZ // 2) + b) * dates_here, dates_here))
                        for i in range(2):
                            a = 2 * b + i
                            for j in range(windows // 2):
                                at = i * (LANES // 2) + j * PATCH_RG
                                z_ref[
                                    u * (windows // 2) + j,
                                    a * PATCH_RG : (a + 1) * PATCH_RG,
                                    part * total : (part + 1) * total,
                                ] = line[at : at + PATCH_RG]
                for i in range(windows // 2 // TOGETHER):
                    whiten(u * (windows // 2 // TOGETHER) + i, 0)

        for a in range(PATCH_AZ):
            flat_ref[pl.ds(a, 2 * total, stride=PATCH_AZ), :] = across(white_ref[a], shift_ref[a * 2 + h])
        for q in range(CHUNKS):
            for to in range(near):
                row_msg[h, to, q] = flat_ref[
                    pl.ds((to * CHUNKS + q) * deep * PATCH_AZ, deep * PATCH_AZ), :
                ].astype(jnp.bfloat16)
            got_rows[h, rank, q] = row_msg[h, rank, q]
            if h == PHASES - 1:
                for k in inner:
                    to = partner(k) % near
                    send(row_msg.at[h, to, q], got_rows.at[h, rank, q], row_send.at[0], row_recv.at[1 + q], partner(k))
        if h < PHASES - 1:
            for k in inner:
                to = partner(k) % near
                send(row_msg.at[h, to], got_rows.at[h, rank], row_send.at[0], row_recv.at[0], partner(k))
            settle()

    drain(got_rows.at[0, pl.ds(0, near - 1)], row_recv.at[0])

    def reduce(q, carry):
        drain(got_rows.at[1, pl.ds(0, near - 1), q], row_recv.at[1 + q])
        for i in range(deep // 2):
            at = slice(i * PAIR, (i + 1) * PAIR)
            cells = jnp.concatenate([got_rows[h, s, q, at, :] for h in range(PHASES) for s in range(near)], axis=0)
            out = jnp.dot(spread_ref[...], cells, preferred_element_type=jnp.float32).astype(jnp.bfloat16)
            for o in range(n):
                sum_msg[q, o, at, :] = out[o * PAIR : (o + 1) * PAIR]
        got_sums[q, me] = sum_msg[q, me]
        for k in peers:
            send(sum_msg.at[q, partner(k)], got_sums.at[q, me], sum_send.at[0], sum_recv.at[q], partner(k))
        return carry

    lax.fori_loop(0, CHUNKS, reduce, 0)

    def finish(q, carry):
        drain(got_sums.at[q, pl.ds(0, n - 1)], sum_recv.at[q])

        for s in range(near):
            y = got_sums[q, s].astype(jnp.float32)
            for k in range(1, GROUPS):
                y = y + got_sums[q, s + k * near].astype(jnp.float32)
            for r in range(deep):
                at = pl.ds((s * CHUNKS + q) * deep + r, MAP_DEV, stride=2 * total)
                result_ref[at, :] = y[r * MAP_DEV : (r + 1) * MAP_DEV] * inv_ref[...]
        return carry

    lax.fori_loop(0, CHUNKS, finish, 0)

    drain(got_facts.at[pl.ds(0, n - 1)], fact_send.at[0])
    drain(cells_ref.at[pl.ds(0, n - 1)], cell_send.at[0])
    drain(split_ref.at[:, pl.ds(0, n - 1)], cell_send.at[1])
    drain(row_msg.at[:, pl.ds(0, near - 1)], row_send.at[0])
    drain(sum_msg.at[:, pl.ds(0, n - 1)], sum_send.at[0])


def shards(n, radar_stack, filter_taps, filter_lengths, resample_kernel, tile_owner, map_slot, correlation, offsets):
    dates_here, rows, ranges = radar_stack.shape[1:]
    dates = n * dates_here
    tile_count = tile_owner.shape[0]
    near = n // GROUPS
    slots = PHASES * near * PAIR
    deep = 2 * dates // near // CHUNKS
    block = (n, 2 * PATCH_AZ * dates_here, LANES)
    split = (2, n, PATCH_AZ * dates_here, LANES)
    row_block = (PHASES, near, CHUNKS, deep * PATCH_AZ, LANES)
    sum_block = (CHUNKS, n, MAP_DEV * deep, LANES)
    facts = [x.reshape(1, tile_count) for x in (tile_owner, map_slot, offsets, correlation)]
    given = (filter_lengths, resample_kernel, radar_stack, filter_taps, *facts)

    dma = pltpu.SemaphoreType.DMA
    result = pl.pallas_call(
        partial(flow_kernel, n),
        out_shape=jax.ShapeDtypeStruct((MAP_DEV * 2 * dates, TILE), jnp.float32),
        in_specs=[HBM] * len(given),
        out_specs=VMEM,
        scratch_shapes=[
            pltpu.VMEM(block, jnp.bfloat16),
            pltpu.VMEM(block, jnp.bfloat16),
            pltpu.VMEM(split, jnp.bfloat16),
            pltpu.VMEM(split, jnp.bfloat16),
            pltpu.VMEM((FACTS, slots), jnp.float32),
            pltpu.VMEM((n, FACTS, slots), jnp.float32),
            pltpu.VMEM(block, jnp.float32),
            pltpu.VMEM((LANES // PATCH_RG, LANES, 2 * dates), jnp.bfloat16),
            pltpu.VMEM((PATCH_AZ, LANES, 2 * dates), jnp.bfloat16),
            pltpu.VMEM((2 * dates * PATCH_AZ, LANES), jnp.float32),
            pltpu.VMEM(row_block, jnp.bfloat16),
            pltpu.VMEM(row_block, jnp.bfloat16),
            pltpu.VMEM(sum_block, jnp.bfloat16),
            pltpu.VMEM(sum_block, jnp.bfloat16),
            pltpu.VMEM((dates_here, 2 * rows, 2 * rows), jnp.bfloat16),
            pltpu.VMEM((n * PAIR, slots), jnp.bfloat16),
            pltpu.VMEM((tile_count, TILE, TILE), jnp.bfloat16),
            pltpu.VMEM((MAP_DEV, LANES), jnp.float32),
            pltpu.VMEM((TOGETHER, dates, 2 * dates), jnp.float32),
            pltpu.VMEM((TOGETHER, LANES, 2 * dates), jnp.float32),
            pltpu.VMEM((TOGETHER, dates + LANES, 2 * dates), jnp.bfloat16),
            pltpu.VMEM((TOGETHER, 2 * dates, 2 * dates), jnp.bfloat16),
            pltpu.SMEM(filter_lengths.shape, jnp.int32),
            pltpu.SMEM(resample_kernel.shape, jnp.float32),
            pltpu.VMEM(radar_stack.shape, radar_stack.dtype),
            pltpu.VMEM(filter_taps.shape, jnp.float32),
            pltpu.VMEM((1, tile_count), jnp.int32),
            pltpu.VMEM((1, tile_count), jnp.int32),
            pltpu.VMEM((1, tile_count), jnp.int32),
            pltpu.VMEM((1, tile_count), jnp.int32),
            dma((3,)),
            dma((1,)),
            dma((1,)),
            dma((2,)),
            dma((3,)),
            dma((1,)),
            dma((1 + CHUNKS,)),
            dma((1,)),
            dma((CHUNKS,)),
            dma((len(given),)),
        ],
        compiler_params=pltpu.CompilerParams(collective_id=0, has_side_effects=True, vmem_limit_bytes=BIG),
        name="flow",
    )(*[pltpu.with_memory_space_constraint(x, pltpu.MemorySpace.HBM) for x in given])
    return result.reshape(MAP_DEV, 2 * dates, TILE)


def solution(mesh):
    in_specs = (
        P(None, "date", "grp", None),
        P(None, "date", None),
        P("date"),
        P(),
        P(("grp", "date"), None),
        P(("grp", "date")),
        P(("grp", "date")),
        P(("grp", "date")),
    )
    out_specs = P(("grp", "date"), None, None)
    return jax.shard_map(
        partial(shards, mesh.shape["date"]), mesh=mesh, in_specs=in_specs, out_specs=out_specs, check_vma=False
    )
```

```python
from functools import partial

import jax
import jax.numpy as jnp
from jax import lax
from jax.experimental import pallas as pl
from jax.experimental.pallas import tpu as pltpu
from jax.sharding import PartitionSpec as P

PATCH_AZ = 8
PATCH_RG = 16
TILE = 128
KW = 4
MAP_DEV = 8
LANES = 128
PHASES = 2
TOGETHER = 4
SWEEPS = 3
GROUPS = 2
CHUNKS = 8
AHEAD = 2
FACTS = 8
PAIR = 2 * PATCH_AZ

diag_load = 0.5
small_eps = 1e-05
MESH = pl.DeviceIdType.MESH
VMEM = pl.BlockSpec(memory_space=pltpu.VMEM)
HBM = pl.BlockSpec(memory_space=pltpu.MemorySpace.HBM)
BIG = 32 * 1024 * 1024


def across(x, y):
    return lax.dot_general(x, y, (((0,), (0,)), ((), ())), preferred_element_type=jnp.float32)


def operator_of(top):
    dates = top.shape[0]
    return jnp.concatenate([top, jnp.concatenate([-top[:, dates:], top[:, :dates]], axis=1)], axis=0)


def whiten_windows(z_ref, first, white_ref, half_ref, cells_ref, left_ref, right_ref):
    looks, dates = z_ref.shape[1], z_ref.shape[2] // 2
    eye = lax.broadcasted_iota(jnp.int32, (dates, dates), 0) == lax.broadcasted_iota(jnp.int32, (dates, dates), 1)
    overs = []
    for q in range(TOGETHER):
        zt = z_ref[first + q]
        zt_re, zt_im = zt[:, :dates], zt[:, dates:]
        top = across(
            jnp.concatenate([zt_re, zt_im], axis=0),
            jnp.concatenate([zt, jnp.concatenate([zt_im, -zt_re], axis=1)], axis=0),
        )
        diagonal = jnp.where(eye, top[:, :dates], 0.0)
        scale_col = lax.rsqrt(jnp.sum(diagonal, axis=1, keepdims=True) * (1.0 / looks) + small_eps) * (1.0 / looks)
        scale_row = lax.rsqrt(jnp.sum(diagonal, axis=0, keepdims=True) * (1.0 / looks) + small_eps)
        outer = scale_col * scale_row
        coher_re = top[:, :dates] * outer + jnp.where(eye, diag_load, 0.0)
        coher_im = top[:, dates:] * outer
        sums = jnp.sum(jnp.abs(coher_re) + jnp.abs(coher_im), axis=0, keepdims=True)
        over = 1.0 / jnp.max(sums, axis=1, keepdims=True)
        half = jnp.concatenate([coher_re, coher_im], axis=1) * (0.5 * over)
        half_ref[q] = half
        rounded = half.astype(jnp.bfloat16)
        left_ref[q] = jnp.concatenate([rounded, zt], axis=0)
        right_ref[q] = operator_of(rounded)
        overs.append(over)
    for stage in range(SWEEPS - 1):
        for q in range(TOGETHER):
            both = jnp.dot(left_ref[q], right_ref[q], preferred_element_type=jnp.float32)
            half = half_ref[q] - both[:dates]
            if stage == 0:
                cells = z_ref[first + q].astype(jnp.float32) - both[dates:]
            else:
                cells = cells_ref[q] - both[dates:]
            rounded = half.astype(jnp.bfloat16)
            if stage < SWEEPS - 2:
                half_ref[q] = half
                left_ref[q, :dates] = rounded
            cells_ref[q] = cells
            left_ref[q, dates:] = cells.astype(jnp.bfloat16)
            right_ref[q] = operator_of(rounded * (2.0 ** (stage + 1)))
    for q in range(TOGETHER):
        applied = jnp.dot(left_ref[q, dates:], right_ref[q], preferred_element_type=jnp.float32)
        white = ((cells_ref[q] - applied) * (2.0**SWEEPS * overs[q])).astype(jnp.bfloat16)
        for a in range(PATCH_AZ):
            white_ref[a, pl.ds((first + q) * PATCH_RG, PATCH_RG), :] = white[a * PATCH_RG : (a + 1) * PATCH_RG]


def flow_kernel(n, *refs):
    inputs, refs = refs[:8], refs[8:]
    result_ref, cells_ref, got_cells, split_ref, got_split, facts_ref, got_facts, cell_ref, z_ref, white_ref, flat_ref = refs[:11]
    row_msg, got_rows, sum_msg, got_sums, operator_ref, spread_ref, shift_ref, inv_ref = refs[11:19]
    work, local, refs = refs[19:23], refs[23:31], refs[31:]
    len_ref, kern_ref, radar_ref, taps_ref = local[:4]
    fact_refs = local[4:8]
    own_sem, fact_send, fact_recv, cell_send, cell_recv, row_send, row_recv, sum_send, sum_recv, load_sem = refs
    me = lax.axis_index("date")
    dates_here, rows = radar_ref.shape[1], radar_ref.shape[2]
    taps, tile_count = taps_ref.shape[2], fact_refs[0].shape[1]
    total = n * dates_here
    windows = LANES // PATCH_RG
    near = n // GROUPS
    group, rank = me // near, me % near
    slots = spread_ref.shape[1]
    deep = 2 * total // near // CHUNKS

    barrier = pltpu.get_barrier_semaphore()
    loads = [pltpu.make_async_copy(x, y, load_sem.at[i]) for i, (x, y) in enumerate(zip(inputs, local))]
    for load in loads:
        load.start()
    for k in range(1, n):
        pl.semaphore_signal(barrier, inc=1, device_id={"date": lax.rem(me + k, n)}, device_id_type=MESH)
    own = [pltpu.make_async_copy(cells_ref.at[me], got_cells.at[me], own_sem.at[0])]
    own += [pltpu.make_async_copy(split_ref.at[u, me], got_split.at[u, me], own_sem.at[1 + u]) for u in range(2)]

    def send(src, dst, send_sem, recv_sem, peer):
        pltpu.make_async_remote_copy(
            src_ref=src,
            dst_ref=dst,
            send_sem=send_sem,
            recv_sem=recv_sem,
            device_id={"date": peer},
            device_id_type=MESH,
        ).start()

    def drain(ref, sem):
        pltpu.make_async_copy(ref, ref, sem).wait()

    def partner(k):
        peer, bit = me, 1
        while bit < n:
            peer = peer + (k // bit) % 2 * (1 - (me // bit) % 2 * 2) * bit
            bit *= 2
        return peer

    def turn(i):
        return n - 1 - i // 2 - i % 2 * (n // 2)

    peers = [turn(i) for i in range(n - 1)]
    inner = list(range(near - 1, 0, -1))

    for load in loads:
        load.wait()
    tiles = slots // 2
    tile_at = lax.broadcasted_iota(jnp.int32, (LANES, tiles), 0)
    lane_at = lax.broadcasted_iota(jnp.int32, (LANES, tiles), 1)
    placed = ((tile_at & 1) * near + rank) * PATCH_AZ + (tile_at >> 1)
    hit = jnp.logical_and(lane_at == placed, tile_at < tile_count)
    moving = jnp.where(hit, 1.0, 0.0).astype(jnp.bfloat16)
    listed = jnp.concatenate([fact_refs[0][...] * MAP_DEV + fact_refs[1][...], fact_refs[3][...]], axis=0)
    listed = jnp.concatenate([listed.astype(jnp.float32), jnp.zeros((2, LANES - tile_count), jnp.float32)], axis=1)
    listed = jnp.concatenate([listed, jnp.zeros((FACTS - 2, LANES), jnp.float32)], axis=0)
    facts_ref[...] = jnp.dot(listed.astype(jnp.bfloat16), moving, preferred_element_type=jnp.float32)[:2]
    position = lax.broadcasted_iota(jnp.int32, (1, taps), 1)
    a_iota = lax.broadcasted_iota(jnp.int32, (rows, rows), 0)
    b_iota = lax.broadcasted_iota(jnp.int32, (rows, rows), 1)
    tap_at = b_iota - a_iota + taps // 2
    inside = jnp.logical_and(tap_at >= 0, tap_at < taps)

    def toeplitz(d, which):
        kept = jnp.where(position < len_ref[d], taps_ref[which, pl.ds(d, 1), :], 0.0)
        rolled = pltpu.roll(jnp.broadcast_to(kept, (rows, taps)), taps // 2, 1, stride=1, stride_axis=0)
        return jnp.where(inside, jnp.concatenate([rolled] * (rows // taps), axis=1), 0.0)

    for h in range(PHASES):
        for d in range(dates_here):
            if h == 0:
                t_re, t_im = toeplitz(d, 0), toeplitz(d, 1)
                operator_ref[d] = jnp.concatenate(
                    [jnp.concatenate([t_re, -t_im], axis=1), jnp.concatenate([t_im, t_re], axis=1)], axis=0
                ).astype(jnp.bfloat16)
            side = slice(h * LANES, (h + 1) * LANES)
            columns = jnp.concatenate([radar_ref[0, d, :, side], radar_ref[1, d, :, side]], axis=0)
            product = jnp.dot(operator_ref[d], columns, preferred_element_type=jnp.float32)
            for p in range(n):
                for part in range(2):
                    top = part * rows + p * PATCH_AZ
                    cell_ref[p, pl.ds(part * PATCH_AZ * dates_here + d, PATCH_AZ, stride=dates_here), :] = product[
                        top : top + PATCH_AZ
                    ]
        if h == 0:
            for p in range(n):
                cells_ref[p] = cell_ref[p].astype(jnp.bfloat16)
            pl.semaphore_wait(barrier, n - 1)
            for k in peers:
                send(facts_ref, got_facts.at[me], fact_send.at[0], fact_recv.at[0], partner(k))
            got_facts[me] = facts_ref[...]
            for k in peers:
                send(cells_ref.at[partner(k)], got_cells.at[me], cell_send.at[0], cell_recv.at[0], partner(k))
            own[0].start()
        else:
            low = lax.broadcasted_iota(jnp.int32, (PATCH_AZ * dates_here, LANES), 1) < LANES // 2
            for p in range(n):
                lines = cell_ref[p].reshape(PATCH_AZ, 2, dates_here, LANES)
                even, odd = [lines[:, i].reshape(PATCH_AZ * dates_here, LANES) for i in range(2)]
                split_ref[0, p] = jnp.where(low, even, pltpu.roll(odd, LANES // 2, 1)).astype(jnp.bfloat16)
                split_ref[1, p] = jnp.where(low, pltpu.roll(even, LANES // 2, 1), odd).astype(jnp.bfloat16)
            for u in range(2):
                for k in peers:
                    send(
                        split_ref.at[u, partner(k)], got_split.at[u, me], cell_send.at[1], cell_recv.at[1 + u], partner(k)
                    )
                own[1 + u].start()

    apart = lax.broadcasted_iota(jnp.int32, (TILE, TILE), 0) - lax.broadcasted_iota(jnp.int32, (TILE, TILE), 1) + TILE
    for t in range(tile_count):
        shift = fact_refs[2][:, t : t + 1]
        step = (apart - shift) & (TILE - 1)
        circ = jnp.zeros((TILE, TILE), jnp.float32)
        for k in range(KW):
            circ = jnp.where(step == k, kern_ref[k], circ)
        shift_ref[t] = circ.astype(jnp.bfloat16)

    def send_rows(q):
        for k in inner:
            to = partner(k) % near
            send(row_msg.at[1, to, q], got_rows.at[1, rank, q], row_send.at[0], row_recv.at[1 + q], partner(k))

    def send_sums(q, ks):
        for k in ks:
            send(sum_msg.at[q, partner(k)], got_sums.at[q, me], sum_send.at[0], sum_recv.at[q], partner(k))

    def settle():
        drain(got_facts.at[pl.ds(0, n - 1)], fact_recv.at[0])
        from_at = lax.broadcasted_iota(jnp.int32, (tiles, slots), 0)
        into_at = lax.broadcasted_iota(jnp.int32, (tiles, slots), 1)
        twice = ((into_at >> 4) * PATCH_AZ + (into_at & (PATCH_AZ - 1))) == from_at
        twice = jnp.where(twice, 1.0, 0.0).astype(jnp.bfloat16)

        def all_of(k):
            facts = got_facts[k * near]
            for s in range(1, near):
                facts = facts + got_facts[k * near + s]
            return facts

        here = jnp.concatenate([all_of(group), jnp.zeros((FACTS - 2, tiles), jnp.float32)], axis=0)
        here = jnp.dot(here.astype(jnp.bfloat16), twice, preferred_element_type=jnp.float32)
        row_at = lax.broadcasted_iota(jnp.int32, spread_ref.shape, 0)
        slot_at = lax.broadcasted_iota(jnp.int32, spread_ref.shape, 1)
        named = ((row_at >> 4) * MAP_DEV + (row_at & 7)).astype(jnp.float32)
        same = jnp.logical_and(named == here[0:1], ((row_at ^ slot_at) & PATCH_AZ) == 0)
        spread_ref[...] = jnp.where(same, here[1:2], 0.0).astype(jnp.bfloat16)
        mine = (me * MAP_DEV + lax.broadcasted_iota(jnp.int32, (MAP_DEV, tiles), 0)).astype(jnp.float32)
        count = jnp.zeros((MAP_DEV, tiles), jnp.float32)
        for k in range(GROUPS):
            facts = all_of(k)
            count = count + jnp.where(mine == facts[0:1], facts[1:2], 0.0)
        inv_ref[...] = jnp.broadcast_to(1.0 / jnp.maximum(jnp.sum(count, axis=1, keepdims=True), 1.0), inv_ref.shape)

    def whiten(i, carry):
        whiten_windows(z_ref, i * TOGETHER, white_ref, *work)
        return carry

    def line_of(at):
        return jnp.concatenate([cell_ref[s, at, :] for s in range(n)], axis=0).T.astype(jnp.bfloat16)

    for h in range(PHASES):
        if h == 0:
            own[0].wait()
            drain(got_cells.at[pl.ds(0, n - 1)], cell_recv.at[0])
            for s in range(n):
                cell_ref[s] = got_cells[s].astype(jnp.float32)
            for part in range(2):
                for a in range(PATCH_AZ):
                    line = line_of(pl.ds((part * PATCH_AZ + a) * dates_here, dates_here))
                    for j in range(windows):
                        z_ref[j, a * PATCH_RG : (a + 1) * PATCH_RG, part * total : (part + 1) * total] = line[
                            j * PATCH_RG : (j + 1) * PATCH_RG
                        ]
            lax.fori_loop(0, windows // TOGETHER, whiten, 0)
        else:
            for u in range(2):
                own[1 + u].wait()
                drain(got_split.at[u, pl.ds(0, n - 1)], cell_recv.at[1 + u])
                for s in range(n):
                    cell_ref[s, : PATCH_AZ * dates_here] = got_split[u, s].astype(jnp.float32)
                for part in range(2):
                    for b in range(PATCH_AZ // 2):
                        line = line_of(pl.ds((part * (PATCH_AZ // 2) + b) * dates_here, dates_here))
                        for i in range(2):
                            a = 2 * b + i
                            for j in range(windows // 2):
                                at = i * (LANES // 2) + j * PATCH_RG
                                z_ref[
                                    u * (windows // 2) + j,
                                    a * PATCH_RG : (a + 1) * PATCH_RG,
                                    part * total : (part + 1) * total,
                                ] = line[at : at + PATCH_RG]
                for i in range(windows // 2 // TOGETHER):
                    whiten(u * (windows // 2 // TOGETHER) + i, 0)

        for a in range(PATCH_AZ):
            flat_ref[pl.ds(a, 2 * total, stride=PATCH_AZ), :] = across(white_ref[a], shift_ref[a * 2 + h])
        for q in range(CHUNKS):
            for to in range(near):
                row_msg[h, to, q] = flat_ref[
                    pl.ds((to * CHUNKS + q) * deep * PATCH_AZ, deep * PATCH_AZ), :
                ].astype(jnp.bfloat16)
            got_rows[h, rank, q] = row_msg[h, rank, q]
            if h == PHASES - 1 and q < AHEAD:
                send_rows(q)
        if h < PHASES - 1:
            for k in inner:
                to = partner(k) % near
                send(row_msg.at[h, to], got_rows.at[h, rank], row_send.at[0], row_recv.at[0], partner(k))
            settle()

    drain(got_rows.at[0, pl.ds(0, near - 1)], row_recv.at[0])

    def reduce(q, carry):
        drain(got_rows.at[1, pl.ds(0, near - 1), q], row_recv.at[1 + q])
        for i in range(deep // 2):
            at = slice(i * PAIR, (i + 1) * PAIR)
            cells = jnp.concatenate([got_rows[h, s, q, at, :] for h in range(PHASES) for s in range(near)], axis=0)
            out = jnp.dot(spread_ref[...], cells, preferred_element_type=jnp.float32).astype(jnp.bfloat16)
            for o in range(n):
                sum_msg[q, o, at, :] = out[o * PAIR : (o + 1) * PAIR]
        got_sums[q, me] = sum_msg[q, me]
        send_sums(q, range(near, n))

        @pl.when(q + AHEAD < CHUNKS)
        def _():
            send_rows(q + AHEAD)

        send_sums(q, inner)
        return carry

    lax.fori_loop(0, CHUNKS, reduce, 0)

    def finish(q, carry):
        drain(got_sums.at[q, pl.ds(0, n - 1)], sum_recv.at[q])

        for s in range(near):
            y = got_sums[q, s].astype(jnp.float32)
            for k in range(1, GROUPS):
                y = y + got_sums[q, s + k * near].astype(jnp.float32)
            for r in range(deep):
                at = pl.ds((s * CHUNKS + q) * deep + r, MAP_DEV, stride=2 * total)
                result_ref[at, :] = y[r * MAP_DEV : (r + 1) * MAP_DEV] * inv_ref[...]
        return carry

    lax.fori_loop(0, CHUNKS, finish, 0)

    drain(got_facts.at[pl.ds(0, n - 1)], fact_send.at[0])
    drain(cells_ref.at[pl.ds(0, n - 1)], cell_send.at[0])
    drain(split_ref.at[:, pl.ds(0, n - 1)], cell_send.at[1])
    drain(row_msg.at[:, pl.ds(0, near - 1)], row_send.at[0])
    drain(sum_msg.at[:, pl.ds(0, n - 1)], sum_send.at[0])


def shards(n, radar_stack, filter_taps, filter_lengths, resample_kernel, tile_owner, map_slot, correlation, offsets):
    dates_here, rows, ranges = radar_stack.shape[1:]
    dates = n * dates_here
    tile_count = tile_owner.shape[0]
    near = n // GROUPS
    slots = PHASES * near * PAIR
    deep = 2 * dates // near // CHUNKS
    block = (n, 2 * PATCH_AZ * dates_here, LANES)
    split = (2, n, PATCH_AZ * dates_here, LANES)
    row_block = (PHASES, near, CHUNKS, deep * PATCH_AZ, LANES)
    sum_block = (CHUNKS, n, MAP_DEV * deep, LANES)
    facts = [x.reshape(1, tile_count) for x in (tile_owner, map_slot, offsets, correlation)]
    given = (filter_lengths, resample_kernel, radar_stack, filter_taps, *facts)

    dma = pltpu.SemaphoreType.DMA
    result = pl.pallas_call(
        partial(flow_kernel, n),
        out_shape=jax.ShapeDtypeStruct((MAP_DEV * 2 * dates, TILE), jnp.float32),
        in_specs=[HBM] * len(given),
        out_specs=VMEM,
        scratch_shapes=[
            pltpu.VMEM(block, jnp.bfloat16),
            pltpu.VMEM(block, jnp.bfloat16),
            pltpu.VMEM(split, jnp.bfloat16),
            pltpu.VMEM(split, jnp.bfloat16),
            pltpu.VMEM((2, slots // 2), jnp.float32),
            pltpu.VMEM((n, 2, slots // 2), jnp.float32),
            pltpu.VMEM(block, jnp.float32),
            pltpu.VMEM((LANES // PATCH_RG, LANES, 2 * dates), jnp.bfloat16),
            pltpu.VMEM((PATCH_AZ, LANES, 2 * dates), jnp.bfloat16),
            pltpu.VMEM((2 * dates * PATCH_AZ, LANES), jnp.float32),
            pltpu.VMEM(row_block, jnp.bfloat16),
            pltpu.VMEM(row_block, jnp.bfloat16),
            pltpu.VMEM(sum_block, jnp.bfloat16),
            pltpu.VMEM(sum_block, jnp.bfloat16),
            pltpu.VMEM((dates_here, 2 * rows, 2 * rows), jnp.bfloat16),
            pltpu.VMEM((n * PAIR, slots), jnp.bfloat16),
            pltpu.VMEM((tile_count, TILE, TILE), jnp.bfloat16),
            pltpu.VMEM((MAP_DEV, LANES), jnp.float32),
            pltpu.VMEM((TOGETHER, dates, 2 * dates), jnp.float32),
            pltpu.VMEM((TOGETHER, LANES, 2 * dates), jnp.float32),
            pltpu.VMEM((TOGETHER, dates + LANES, 2 * dates), jnp.bfloat16),
            pltpu.VMEM((TOGETHER, 2 * dates, 2 * dates), jnp.bfloat16),
            pltpu.SMEM(filter_lengths.shape, jnp.int32),
            pltpu.SMEM(resample_kernel.shape, jnp.float32),
            pltpu.VMEM(radar_stack.shape, radar_stack.dtype),
            pltpu.VMEM(filter_taps.shape, jnp.float32),
            pltpu.VMEM((1, tile_count), jnp.int32),
            pltpu.VMEM((1, tile_count), jnp.int32),
            pltpu.VMEM((1, tile_count), jnp.int32),
            pltpu.VMEM((1, tile_count), jnp.int32),
            dma((3,)),
            dma((1,)),
            dma((1,)),
            dma((2,)),
            dma((3,)),
            dma((1,)),
            dma((1 + CHUNKS,)),
            dma((1,)),
            dma((CHUNKS,)),
            dma((len(given),)),
        ],
        compiler_params=pltpu.CompilerParams(collective_id=0, has_side_effects=True, vmem_limit_bytes=BIG),
        name="flow",
    )(*[pltpu.with_memory_space_constraint(x, pltpu.MemorySpace.HBM) for x in given])
    return result.reshape(MAP_DEV, 2 * dates, TILE)


def solution(mesh):
    in_specs = (
        P(None, "date", "grp", None),
        P(None, "date", None),
        P("date"),
        P(),
        P(("grp", "date"), None),
        P(("grp", "date")),
        P(("grp", "date")),
        P(("grp", "date")),
    )
    out_specs = P(("grp", "date"), None, None)
    return jax.shard_map(
        partial(shards, mesh.shape["date"]), mesh=mesh, in_specs=in_specs, out_specs=out_specs, check_vma=False
    )
```

```python
from functools import partial

import jax
import jax.numpy as jnp
from jax import lax
from jax.experimental import pallas as pl
from jax.experimental.pallas import tpu as pltpu
from jax.sharding import PartitionSpec as P

PATCH_AZ = 8
PATCH_RG = 16
TILE = 128
KW = 4
MAP_DEV = 8
LANES = 128
PHASES = 2
TOGETHER = 4
SWEEPS = 3
GROUPS = 2
CHUNKS = 4
AHEAD = 2
WIDE = 4
FACTS = 8
PAIR = 2 * PATCH_AZ

diag_load = 0.5
small_eps = 1e-05
MESH = pl.DeviceIdType.MESH
VMEM = pl.BlockSpec(memory_space=pltpu.VMEM)
HBM = pl.BlockSpec(memory_space=pltpu.MemorySpace.HBM)
BIG = 32 * 1024 * 1024


def across(x, y):
    return lax.dot_general(x, y, (((0,), (0,)), ((), ())), preferred_element_type=jnp.float32)


def operator_of(top):
    dates = top.shape[0]
    return jnp.concatenate([top, jnp.concatenate([-top[:, dates:], top[:, :dates]], axis=1)], axis=0)


def whiten_windows(z_ref, first, white_ref, half_ref, cells_ref, left_ref, right_ref):
    looks, dates = z_ref.shape[1], z_ref.shape[2] // 2
    eye = lax.broadcasted_iota(jnp.int32, (dates, dates), 0) == lax.broadcasted_iota(jnp.int32, (dates, dates), 1)
    overs = []
    for q in range(TOGETHER):
        zt = z_ref[first + q]
        zt_re, zt_im = zt[:, :dates], zt[:, dates:]
        top = across(
            jnp.concatenate([zt_re, zt_im], axis=0),
            jnp.concatenate([zt, jnp.concatenate([zt_im, -zt_re], axis=1)], axis=0),
        )
        diagonal = jnp.where(eye, top[:, :dates], 0.0)
        scale_col = lax.rsqrt(jnp.sum(diagonal, axis=1, keepdims=True) * (1.0 / looks) + small_eps) * (1.0 / looks)
        scale_row = lax.rsqrt(jnp.sum(diagonal, axis=0, keepdims=True) * (1.0 / looks) + small_eps)
        outer = scale_col * scale_row
        coher_re = top[:, :dates] * outer + jnp.where(eye, diag_load, 0.0)
        coher_im = top[:, dates:] * outer
        sums = jnp.sum(jnp.abs(coher_re) + jnp.abs(coher_im), axis=0, keepdims=True)
        over = 1.0 / jnp.max(sums, axis=1, keepdims=True)
        half = jnp.concatenate([coher_re, coher_im], axis=1) * (0.5 * over)
        half_ref[q] = half
        rounded = half.astype(jnp.bfloat16)
        left_ref[q] = jnp.concatenate([rounded, zt], axis=0)
        right_ref[q] = operator_of(rounded)
        overs.append(over)
    for stage in range(SWEEPS - 1):
        for q in range(TOGETHER):
            both = jnp.dot(left_ref[q], right_ref[q], preferred_element_type=jnp.float32)
            half = half_ref[q] - both[:dates]
            if stage == 0:
                cells = z_ref[first + q].astype(jnp.float32) - both[dates:]
            else:
                cells = cells_ref[q] - both[dates:]
            rounded = half.astype(jnp.bfloat16)
            if stage < SWEEPS - 2:
                half_ref[q] = half
                left_ref[q, :dates] = rounded
            cells_ref[q] = cells
            left_ref[q, dates:] = cells.astype(jnp.bfloat16)
            right_ref[q] = operator_of(rounded * (2.0 ** (stage + 1)))
    for q in range(TOGETHER):
        applied = jnp.dot(left_ref[q, dates:], right_ref[q], preferred_element_type=jnp.float32)
        white = ((cells_ref[q] - applied) * (2.0**SWEEPS * overs[q])).astype(jnp.bfloat16)
        for a in range(PATCH_AZ):
            white_ref[a, pl.ds((first + q) * PATCH_RG, PATCH_RG), :] = white[a * PATCH_RG : (a + 1) * PATCH_RG]


def flow_kernel(n, *refs):
    inputs, refs = refs[:8], refs[8:]
    result_ref, cells_ref, got_cells, split_ref, got_split, facts_ref, got_facts, cell_ref, z_ref, white_ref, flat_ref = refs[:11]
    row_msg, got_rows, sum_msg, got_sums, operator_ref, spread_ref, shift_ref, inv_ref = refs[11:19]
    wide_msg, got_wide, full_msg, got_full = refs[19:23]
    work, local, refs = refs[23:27], refs[27:35], refs[35:]
    len_ref, kern_ref, radar_ref, taps_ref = local[:4]
    fact_refs = local[4:8]
    own_sem, fact_send, fact_recv, cell_send, cell_recv, row_send, row_recv, sum_send, sum_recv, wide_send, wide_recv, load_sem = refs
    me = lax.axis_index("date")
    dates_here, rows = radar_ref.shape[1], radar_ref.shape[2]
    taps, tile_count = taps_ref.shape[2], fact_refs[0].shape[1]
    total = n * dates_here
    windows = LANES // PATCH_RG
    near = n // GROUPS
    group, rank = me // near, me % near
    slots = spread_ref.shape[2]
    deep = (2 * total - n * WIDE) // near // CHUNKS
    start = n * WIDE

    barrier = pltpu.get_barrier_semaphore()
    loads = [pltpu.make_async_copy(x, y, load_sem.at[i]) for i, (x, y) in enumerate(zip(inputs, local))]
    for load in loads:
        load.start()
    for k in range(1, n):
        pl.semaphore_signal(barrier, inc=1, device_id={"date": lax.rem(me + k, n)}, device_id_type=MESH)
    own = [pltpu.make_async_copy(cells_ref.at[me], got_cells.at[me], own_sem.at[0])]
    own += [pltpu.make_async_copy(split_ref.at[u, me], got_split.at[u, me], own_sem.at[1 + u]) for u in range(2)]

    def send(src, dst, send_sem, recv_sem, peer):
        pltpu.make_async_remote_copy(
            src_ref=src,
            dst_ref=dst,
            send_sem=send_sem,
            recv_sem=recv_sem,
            device_id={"date": peer},
            device_id_type=MESH,
        ).start()

    def drain(ref, sem):
        pltpu.make_async_copy(ref, ref, sem).wait()

    def partner(k):
        peer, bit = me, 1
        while bit < n:
            peer = peer + (k // bit) % 2 * (1 - (me // bit) % 2 * 2) * bit
            bit *= 2
        return peer

    def turn(i):
        return n - 1 - i // 2 - i % 2 * (n // 2)

    peers = [turn(i) for i in range(n - 1)]
    inner = list(range(near - 1, 0, -1))

    for load in loads:
        load.wait()
    tiles = slots // 2
    tile_at = lax.broadcasted_iota(jnp.int32, (LANES, tiles), 0)
    lane_at = lax.broadcasted_iota(jnp.int32, (LANES, tiles), 1)
    placed = ((tile_at & 1) * near + rank) * PATCH_AZ + (tile_at >> 1)
    hit = jnp.logical_and(lane_at == placed, tile_at < tile_count)
    moving = jnp.where(hit, 1.0, 0.0).astype(jnp.bfloat16)
    listed = jnp.concatenate([fact_refs[0][...] * MAP_DEV + fact_refs[1][...], fact_refs[3][...]], axis=0)
    listed = jnp.concatenate([listed.astype(jnp.float32), jnp.zeros((2, LANES - tile_count), jnp.float32)], axis=1)
    listed = jnp.concatenate([listed, jnp.zeros((FACTS - 2, LANES), jnp.float32)], axis=0)
    facts_ref[...] = jnp.dot(listed.astype(jnp.bfloat16), moving, preferred_element_type=jnp.float32)[:2]
    position = lax.broadcasted_iota(jnp.int32, (1, taps), 1)
    a_iota = lax.broadcasted_iota(jnp.int32, (rows, rows), 0)
    b_iota = lax.broadcasted_iota(jnp.int32, (rows, rows), 1)
    tap_at = b_iota - a_iota + taps // 2
    inside = jnp.logical_and(tap_at >= 0, tap_at < taps)

    def toeplitz(d, which):
        kept = jnp.where(position < len_ref[d], taps_ref[which, pl.ds(d, 1), :], 0.0)
        rolled = pltpu.roll(jnp.broadcast_to(kept, (rows, taps)), taps // 2, 1, stride=1, stride_axis=0)
        return jnp.where(inside, jnp.concatenate([rolled] * (rows // taps), axis=1), 0.0)

    for h in range(PHASES):
        for d in range(dates_here):
            if h == 0:
                t_re, t_im = toeplitz(d, 0), toeplitz(d, 1)
                operator_ref[d] = jnp.concatenate(
                    [jnp.concatenate([t_re, -t_im], axis=1), jnp.concatenate([t_im, t_re], axis=1)], axis=0
                ).astype(jnp.bfloat16)
            side = slice(h * LANES, (h + 1) * LANES)
            columns = jnp.concatenate([radar_ref[0, d, :, side], radar_ref[1, d, :, side]], axis=0)
            product = jnp.dot(operator_ref[d], columns, preferred_element_type=jnp.float32)
            for p in range(n):
                for part in range(2):
                    top = part * rows + p * PATCH_AZ
                    cell_ref[p, pl.ds(part * PATCH_AZ * dates_here + d, PATCH_AZ, stride=dates_here), :] = product[
                        top : top + PATCH_AZ
                    ]
        if h == 0:
            for p in range(n):
                cells_ref[p] = cell_ref[p].astype(jnp.bfloat16)
            pl.semaphore_wait(barrier, n - 1)
            for k in peers:
                send(facts_ref, got_facts.at[me], fact_send.at[0], fact_recv.at[0], partner(k))
            got_facts[me] = facts_ref[...]
            for k in peers:
                send(cells_ref.at[partner(k)], got_cells.at[me], cell_send.at[0], cell_recv.at[0], partner(k))
            own[0].start()
        else:
            low = lax.broadcasted_iota(jnp.int32, (PATCH_AZ * dates_here, LANES), 1) < LANES // 2
            for p in range(n):
                lines = cell_ref[p].reshape(PATCH_AZ, 2, dates_here, LANES)
                even, odd = [lines[:, i].reshape(PATCH_AZ * dates_here, LANES) for i in range(2)]
                split_ref[0, p] = jnp.where(low, even, pltpu.roll(odd, LANES // 2, 1)).astype(jnp.bfloat16)
                split_ref[1, p] = jnp.where(low, pltpu.roll(even, LANES // 2, 1), odd).astype(jnp.bfloat16)
            for u in range(2):
                for k in peers:
                    send(
                        split_ref.at[u, partner(k)], got_split.at[u, me], cell_send.at[1], cell_recv.at[1 + u], partner(k)
                    )
                own[1 + u].start()

    apart = lax.broadcasted_iota(jnp.int32, (TILE, TILE), 0) - lax.broadcasted_iota(jnp.int32, (TILE, TILE), 1) + TILE
    for t in range(tile_count):
        shift = fact_refs[2][:, t : t + 1]
        step = (apart - shift) & (TILE - 1)
        circ = jnp.zeros((TILE, TILE), jnp.float32)
        for k in range(KW):
            circ = jnp.where(step == k, kern_ref[k], circ)
        shift_ref[t] = circ.astype(jnp.bfloat16)

    def send_rows(q):
        for k in inner:
            to = partner(k) % near
            send(row_msg.at[1, to, q], got_rows.at[1, rank, q], row_send.at[0], row_recv.at[1 + q], partner(k))

    def send_sums(q, ks):
        for k in ks:
            send(sum_msg.at[q, partner(k)], got_sums.at[q, me], sum_send.at[0], sum_recv.at[q], partner(k))

    def send_wide(h, ks):
        for k in ks:
            send(wide_msg.at[h, partner(k)], got_wide.at[h, me], wide_send.at[0], wide_recv.at[h], partner(k))

    def settle():
        drain(got_facts.at[pl.ds(0, n - 1)], fact_recv.at[0])
        from_at = lax.broadcasted_iota(jnp.int32, (tiles, slots), 0)
        into_at = lax.broadcasted_iota(jnp.int32, (tiles, slots), 1)
        twice = ((into_at >> 4) * PATCH_AZ + (into_at & (PATCH_AZ - 1))) == from_at
        twice = jnp.where(twice, 1.0, 0.0).astype(jnp.bfloat16)

        def all_of(k):
            facts = got_facts[k * near]
            for s in range(1, near):
                facts = facts + got_facts[k * near + s]
            return facts

        row_at = lax.broadcasted_iota(jnp.int32, spread_ref.shape[1:], 0)
        slot_at = lax.broadcasted_iota(jnp.int32, spread_ref.shape[1:], 1)
        named = ((row_at >> 4) * MAP_DEV + (row_at & 7)).astype(jnp.float32)
        for k in range(GROUPS):
            here = jnp.concatenate([all_of(k), jnp.zeros((FACTS - 2, tiles), jnp.float32)], axis=0)
            here = jnp.dot(here.astype(jnp.bfloat16), twice, preferred_element_type=jnp.float32)
            same = jnp.logical_and(named == here[0:1], ((row_at ^ slot_at) & PATCH_AZ) == 0)
            spread_ref[k] = jnp.where(same, here[1:2], 0.0).astype(jnp.bfloat16)
        mine = (me * MAP_DEV + lax.broadcasted_iota(jnp.int32, (MAP_DEV, tiles), 0)).astype(jnp.float32)
        count = jnp.zeros((MAP_DEV, tiles), jnp.float32)
        for k in range(GROUPS):
            facts = all_of(k)
            count = count + jnp.where(mine == facts[0:1], facts[1:2], 0.0)
        inv_ref[...] = jnp.broadcast_to(1.0 / jnp.maximum(jnp.sum(count, axis=1, keepdims=True), 1.0), inv_ref.shape)

    def whiten(i, carry):
        whiten_windows(z_ref, i * TOGETHER, white_ref, *work)
        return carry

    def line_of(at):
        return jnp.concatenate([cell_ref[s, at, :] for s in range(n)], axis=0).T.astype(jnp.bfloat16)

    for h in range(PHASES):
        if h == 0:
            own[0].wait()
            drain(got_cells.at[pl.ds(0, n - 1)], cell_recv.at[0])
            for s in range(n):
                cell_ref[s] = got_cells[s].astype(jnp.float32)
            for part in range(2):
                for a in range(PATCH_AZ):
                    line = line_of(pl.ds((part * PATCH_AZ + a) * dates_here, dates_here))
                    for j in range(windows):
                        z_ref[j, a * PATCH_RG : (a + 1) * PATCH_RG, part * total : (part + 1) * total] = line[
                            j * PATCH_RG : (j + 1) * PATCH_RG
                        ]
            lax.fori_loop(0, windows // TOGETHER, whiten, 0)
        else:
            for u in range(2):
                own[1 + u].wait()
                drain(got_split.at[u, pl.ds(0, n - 1)], cell_recv.at[1 + u])
                if u == 1:
                    send_wide(0, range(n - 1, 0, -1))
                for s in range(n):
                    cell_ref[s, : PATCH_AZ * dates_here] = got_split[u, s].astype(jnp.float32)
                for part in range(2):
                    for b in range(PATCH_AZ // 2):
                        line = line_of(pl.ds((part * (PATCH_AZ // 2) + b) * dates_here, dates_here))
                        for i in range(2):
                            a = 2 * b + i
                            for j in range(windows // 2):
                                at = i * (LANES // 2) + j * PATCH_RG
                                z_ref[
                                    u * (windows // 2) + j,
                                    a * PATCH_RG : (a + 1) * PATCH_RG,
                                    part * total : (part + 1) * total,
                                ] = line[at : at + PATCH_RG]
                for i in range(windows // 2 // TOGETHER):
                    whiten(u * (windows // 2 // TOGETHER) + i, 0)

        for a in range(PATCH_AZ):
            flat_ref[pl.ds(a, 2 * total, stride=PATCH_AZ), :] = across(white_ref[a], shift_ref[a * 2 + h])
        for o in range(n):
            wide_msg[h, o] = flat_ref[pl.ds(o * WIDE * PATCH_AZ, WIDE * PATCH_AZ), :].astype(jnp.bfloat16)
        got_wide[h, me] = wide_msg[h, me]
        for q in range(CHUNKS):
            for to in range(near):
                row_msg[h, to, q] = flat_ref[
                    pl.ds((start + (to * CHUNKS + q) * deep) * PATCH_AZ, deep * PATCH_AZ), :
                ].astype(jnp.bfloat16)
            got_rows[h, rank, q] = row_msg[h, rank, q]
            if h == PHASES - 1 and q < AHEAD:
                send_rows(q)
                if q == 0:
                    send_wide(1, range(n - 1, 0, -1))
        if h < PHASES - 1:
            for k in inner:
                to = partner(k) % near
                send(row_msg.at[h, to], got_rows.at[h, rank], row_send.at[0], row_recv.at[0], partner(k))
            settle()

    drain(got_rows.at[0, pl.ds(0, near - 1)], row_recv.at[0])

    def reduce(q, carry):
        drain(got_rows.at[1, pl.ds(0, near - 1), q], row_recv.at[1 + q])
        for i in range(deep // 2):
            at = slice(i * PAIR, (i + 1) * PAIR)
            cells = jnp.concatenate([got_rows[h, s, q, at, :] for h in range(PHASES) for s in range(near)], axis=0)
            out = jnp.dot(spread_ref[group], cells, preferred_element_type=jnp.float32).astype(jnp.bfloat16)
            for o in range(n):
                sum_msg[q, o, at, :] = out[o * PAIR : (o + 1) * PAIR]
        got_sums[q, me] = sum_msg[q, me]
        send_sums(q, range(near, n))

        @pl.when(q + AHEAD < CHUNKS)
        def _():
            send_rows(q + AHEAD)

        send_sums(q, inner)
        return carry

    def whole():
        for h in range(PHASES):
            drain(got_wide.at[h, pl.ds(0, n - 1)], wide_recv.at[h])
        for i in range(WIDE // 2):
            at = slice(i * PAIR, (i + 1) * PAIR)
            out = jnp.zeros((n * PAIR, LANES), jnp.float32)
            for k in range(GROUPS):
                cells = jnp.concatenate(
                    [got_wide[h, k * near + s, at, :] for h in range(PHASES) for s in range(near)], axis=0
                )
                out = out + jnp.dot(spread_ref[k], cells, preferred_element_type=jnp.float32)
            for o in range(n):
                full_msg[o, at, :] = out[o * PAIR : (o + 1) * PAIR].astype(jnp.bfloat16)
        got_full[me] = full_msg[me]
        for k in range(n - 1, 0, -1):
            send(full_msg.at[partner(k)], got_full.at[me], wide_send.at[1], wide_recv.at[PHASES], partner(k))

    lax.fori_loop(0, 2, reduce, 0)
    whole()
    lax.fori_loop(2, CHUNKS, reduce, 0)

    def finish(q, carry):
        drain(got_sums.at[q, pl.ds(0, n - 1)], sum_recv.at[q])

        for s in range(near):
            y = got_sums[q, s].astype(jnp.float32)
            for k in range(1, GROUPS):
                y = y + got_sums[q, s + k * near].astype(jnp.float32)
            for r in range(deep):
                at = pl.ds(start + (s * CHUNKS + q) * deep + r, MAP_DEV, stride=2 * total)
                result_ref[at, :] = y[r * MAP_DEV : (r + 1) * MAP_DEV] * inv_ref[...]
        return carry

    lax.fori_loop(0, CHUNKS - 1, finish, 0)
    drain(got_full.at[pl.ds(0, n - 1)], wide_recv.at[PHASES])
    for s in range(n):
        y = got_full[s].astype(jnp.float32)
        for r in range(WIDE):
            at = pl.ds(s * WIDE + r, MAP_DEV, stride=2 * total)
            result_ref[at, :] = y[r * MAP_DEV : (r + 1) * MAP_DEV] * inv_ref[...]
    finish(CHUNKS - 1, 0)

    drain(got_facts.at[pl.ds(0, n - 1)], fact_send.at[0])
    drain(cells_ref.at[pl.ds(0, n - 1)], cell_send.at[0])
    drain(split_ref.at[:, pl.ds(0, n - 1)], cell_send.at[1])
    drain(row_msg.at[:, pl.ds(0, near - 1)], row_send.at[0])
    drain(sum_msg.at[:, pl.ds(0, n - 1)], sum_send.at[0])
    drain(wide_msg.at[:, pl.ds(0, n - 1)], wide_send.at[0])
    drain(full_msg.at[pl.ds(0, n - 1)], wide_send.at[1])


def shards(n, radar_stack, filter_taps, filter_lengths, resample_kernel, tile_owner, map_slot, correlation, offsets):
    dates_here, rows, ranges = radar_stack.shape[1:]
    dates = n * dates_here
    tile_count = tile_owner.shape[0]
    near = n // GROUPS
    slots = PHASES * near * PAIR
    deep = (2 * dates - n * WIDE) // near // CHUNKS
    block = (n, 2 * PATCH_AZ * dates_here, LANES)
    split = (2, n, PATCH_AZ * dates_here, LANES)
    row_block = (PHASES, near, CHUNKS, deep * PATCH_AZ, LANES)
    sum_block = (CHUNKS, n, MAP_DEV * deep, LANES)
    facts = [x.reshape(1, tile_count) for x in (tile_owner, map_slot, offsets, correlation)]
    given = (filter_lengths, resample_kernel, radar_stack, filter_taps, *facts)

    dma = pltpu.SemaphoreType.DMA
    result = pl.pallas_call(
        partial(flow_kernel, n),
        out_shape=jax.ShapeDtypeStruct((MAP_DEV * 2 * dates, TILE), jnp.float32),
        in_specs=[HBM] * len(given),
        out_specs=VMEM,
        scratch_shapes=[
            pltpu.VMEM(block, jnp.bfloat16),
            pltpu.VMEM(block, jnp.bfloat16),
            pltpu.VMEM(split, jnp.bfloat16),
            pltpu.VMEM(split, jnp.bfloat16),
            pltpu.VMEM((2, slots // 2), jnp.float32),
            pltpu.VMEM((n, 2, slots // 2), jnp.float32),
            pltpu.VMEM(block, jnp.float32),
            pltpu.VMEM((LANES // PATCH_RG, LANES, 2 * dates), jnp.bfloat16),
            pltpu.VMEM((PATCH_AZ, LANES, 2 * dates), jnp.bfloat16),
            pltpu.VMEM((2 * dates * PATCH_AZ, LANES), jnp.float32),
            pltpu.VMEM(row_block, jnp.bfloat16),
            pltpu.VMEM(row_block, jnp.bfloat16),
            pltpu.VMEM(sum_block, jnp.bfloat16),
            pltpu.VMEM(sum_block, jnp.bfloat16),
            pltpu.VMEM((dates_here, 2 * rows, 2 * rows), jnp.bfloat16),
            pltpu.VMEM((GROUPS, n * PAIR, slots), jnp.bfloat16),
            pltpu.VMEM((tile_count, TILE, TILE), jnp.bfloat16),
            pltpu.VMEM((MAP_DEV, LANES), jnp.float32),
            pltpu.VMEM((PHASES, n, WIDE * PATCH_AZ, LANES), jnp.bfloat16),
            pltpu.VMEM((PHASES, n, WIDE * PATCH_AZ, LANES), jnp.bfloat16),
            pltpu.VMEM((n, WIDE * MAP_DEV, LANES), jnp.bfloat16),
            pltpu.VMEM((n, WIDE * MAP_DEV, LANES), jnp.bfloat16),
            pltpu.VMEM((TOGETHER, dates, 2 * dates), jnp.float32),
            pltpu.VMEM((TOGETHER, LANES, 2 * dates), jnp.float32),
            pltpu.VMEM((TOGETHER, dates + LANES, 2 * dates), jnp.bfloat16),
            pltpu.VMEM((TOGETHER, 2 * dates, 2 * dates), jnp.bfloat16),
            pltpu.SMEM(filter_lengths.shape, jnp.int32),
            pltpu.SMEM(resample_kernel.shape, jnp.float32),
            pltpu.VMEM(radar_stack.shape, radar_stack.dtype),
            pltpu.VMEM(filter_taps.shape, jnp.float32),
            pltpu.VMEM((1, tile_count), jnp.int32),
            pltpu.VMEM((1, tile_count), jnp.int32),
            pltpu.VMEM((1, tile_count), jnp.int32),
            pltpu.VMEM((1, tile_count), jnp.int32),
            dma((3,)),
            dma((1,)),
            dma((1,)),
            dma((2,)),
            dma((3,)),
            dma((1,)),
            dma((1 + CHUNKS,)),
            dma((1,)),
            dma((CHUNKS,)),
            dma((2,)),
            dma((PHASES + 1,)),
            dma((len(given),)),
        ],
        compiler_params=pltpu.CompilerParams(collective_id=0, has_side_effects=True, vmem_limit_bytes=BIG),
        name="flow",
    )(*[pltpu.with_memory_space_constraint(x, pltpu.MemorySpace.HBM) for x in given])
    return result.reshape(MAP_DEV, 2 * dates, TILE)


def solution(mesh):
    in_specs = (
        P(None, "date", "grp", None),
        P(None, "date", None),
        P("date"),
        P(),
        P(("grp", "date"), None),
        P(("grp", "date")),
        P(("grp", "date")),
        P(("grp", "date")),
    )
    out_specs = P(("grp", "date"), None, None)
    return jax.shard_map(
        partial(shards, mesh.shape["date"]), mesh=mesh, in_specs=in_specs, out_specs=out_specs, check_vma=False
    )
```

```python
from functools import partial

import jax
import jax.numpy as jnp
from jax import lax
from jax.experimental import pallas as pl
from jax.experimental.pallas import tpu as pltpu
from jax.sharding import PartitionSpec as P

PATCH_AZ = 8
PATCH_RG = 16
TILE = 128
KW = 4
MAP_DEV = 8
LANES = 128
PHASES = 2
TOGETHER = 4
SWEEPS = 3
GROUPS = 2
CHUNKS = 4
AHEAD = 3
WIDE = 4
FACTS = 8
PAIR = 2 * PATCH_AZ

diag_load = 0.5
small_eps = 1e-05
MESH = pl.DeviceIdType.MESH
VMEM = pl.BlockSpec(memory_space=pltpu.VMEM)
HBM = pl.BlockSpec(memory_space=pltpu.MemorySpace.HBM)
BIG = 32 * 1024 * 1024


def across(x, y):
    return lax.dot_general(x, y, (((0,), (0,)), ((), ())), preferred_element_type=jnp.float32)


def operator_of(top):
    dates = top.shape[0]
    return jnp.concatenate([top, jnp.concatenate([-top[:, dates:], top[:, :dates]], axis=1)], axis=0)


def whiten_windows(z_ref, first, white_ref, half_ref, cells_ref, left_ref, right_ref):
    looks, dates = z_ref.shape[1], z_ref.shape[2] // 2
    eye = lax.broadcasted_iota(jnp.int32, (dates, dates), 0) == lax.broadcasted_iota(jnp.int32, (dates, dates), 1)
    overs = []
    for q in range(TOGETHER):
        zt = z_ref[first + q]
        zt_re, zt_im = zt[:, :dates], zt[:, dates:]
        top = across(
            jnp.concatenate([zt_re, zt_im], axis=0),
            jnp.concatenate([zt, jnp.concatenate([zt_im, -zt_re], axis=1)], axis=0),
        )
        diagonal = jnp.where(eye, top[:, :dates], 0.0)
        scale_col = lax.rsqrt(jnp.sum(diagonal, axis=1, keepdims=True) * (1.0 / looks) + small_eps) * (1.0 / looks)
        scale_row = lax.rsqrt(jnp.sum(diagonal, axis=0, keepdims=True) * (1.0 / looks) + small_eps)
        outer = scale_col * scale_row
        coher_re = top[:, :dates] * outer + jnp.where(eye, diag_load, 0.0)
        coher_im = top[:, dates:] * outer
        sums = jnp.sum(jnp.abs(coher_re) + jnp.abs(coher_im), axis=0, keepdims=True)
        over = 1.0 / jnp.max(sums, axis=1, keepdims=True)
        half = jnp.concatenate([coher_re, coher_im], axis=1) * (0.5 * over)
        half_ref[q] = half
        rounded = half.astype(jnp.bfloat16)
        left_ref[q] = jnp.concatenate([rounded, zt], axis=0)
        right_ref[q] = operator_of(rounded)
        overs.append(over)
    for stage in range(SWEEPS - 1):
        for q in range(TOGETHER):
            both = jnp.dot(left_ref[q], right_ref[q], preferred_element_type=jnp.float32)
            half = half_ref[q] - both[:dates]
            if stage == 0:
                cells = z_ref[first + q].astype(jnp.float32) - both[dates:]
            else:
                cells = cells_ref[q] - both[dates:]
            rounded = half.astype(jnp.bfloat16)
            if stage < SWEEPS - 2:
                half_ref[q] = half
                left_ref[q, :dates] = rounded
            cells_ref[q] = cells
            left_ref[q, dates:] = cells.astype(jnp.bfloat16)
            right_ref[q] = operator_of(rounded * (2.0 ** (stage + 1)))
    for q in range(TOGETHER):
        applied = jnp.dot(left_ref[q, dates:], right_ref[q], preferred_element_type=jnp.float32)
        white = ((cells_ref[q] - applied) * (2.0**SWEEPS * overs[q])).astype(jnp.bfloat16)
        for a in range(PATCH_AZ):
            white_ref[a, pl.ds((first + q) * PATCH_RG, PATCH_RG), :] = white[a * PATCH_RG : (a + 1) * PATCH_RG]


def flow_kernel(n, *refs):
    inputs, refs = refs[:8], refs[8:]
    result_ref, cells_ref, got_cells, split_ref, got_split, facts_ref, got_facts, cell_ref, z_ref, white_ref, flat_ref = refs[:11]
    row_msg, got_rows, sum_msg, got_sums, operator_ref, spread_ref, shift_ref, inv_ref = refs[11:19]
    wide_msg, got_wide, full_msg, got_full = refs[19:23]
    work, local, refs = refs[23:27], refs[27:35], refs[35:]
    len_ref, kern_ref, radar_ref, taps_ref = local[:4]
    fact_refs = local[4:8]
    own_sem, fact_send, fact_recv, cell_send, cell_recv, row_send, row_recv, sum_send, sum_recv, wide_send, wide_recv, load_sem, ready_sem = refs
    me = lax.axis_index("date")
    dates_here, rows = radar_ref.shape[1], radar_ref.shape[2]
    taps, tile_count = taps_ref.shape[2], fact_refs[0].shape[1]
    total = n * dates_here
    windows = LANES // PATCH_RG
    near = n // GROUPS
    group, rank = me // near, me % near
    slots = spread_ref.shape[2]
    deep = (2 * total - n * WIDE) // near // CHUNKS
    start = n * WIDE

    barrier = pltpu.get_barrier_semaphore()
    loads = [pltpu.make_async_copy(x, y, load_sem.at[i]) for i, (x, y) in enumerate(zip(inputs, local))]
    for load in loads:
        load.start()
    own = [pltpu.make_async_copy(cells_ref.at[me], got_cells.at[me], own_sem.at[0])]
    own += [pltpu.make_async_copy(split_ref.at[u, me], got_split.at[u, me], own_sem.at[1 + u]) for u in range(2)]

    def send(src, dst, send_sem, recv_sem, peer):
        pltpu.make_async_remote_copy(
            src_ref=src,
            dst_ref=dst,
            send_sem=send_sem,
            recv_sem=recv_sem,
            device_id={"date": peer},
            device_id_type=MESH,
        ).start()

    def drain(ref, sem):
        pltpu.make_async_copy(ref, ref, sem).wait()

    def partner(k):
        peer, bit = me, 1
        while bit < n:
            peer = peer + (k // bit) % 2 * (1 - (me // bit) % 2 * 2) * bit
            bit *= 2
        return peer

    def turn(i):
        return n - 1 - i // 2 - i % 2 * (n // 2)

    quarter = n // 4
    middle = (me // quarter) % 2 != me // (2 * quarter)
    close = list(range(1, 2 * quarter))
    beside = list(range(3 * quarter, n))
    apart = list(range(2 * quarter, 3 * quarter))

    def tell(sem, k):
        pl.semaphore_signal(sem, inc=1, device_id={"date": partner(k)}, device_id_type=MESH)

    for k in close:
        tell(barrier, k)

    @pl.when(middle)
    def _():
        for k in beside:
            tell(barrier, k)

    peers = [turn(i) for i in range(n - 1)]
    inner = list(range(near - 1, 0, -1))

    for load in loads:
        load.wait()
    tiles = slots // 2
    tile_at = lax.broadcasted_iota(jnp.int32, (LANES, tiles), 0)
    lane_at = lax.broadcasted_iota(jnp.int32, (LANES, tiles), 1)
    placed = ((tile_at & 1) * near + rank) * PATCH_AZ + (tile_at >> 1)
    hit = jnp.logical_and(lane_at == placed, tile_at < tile_count)
    moving = jnp.where(hit, 1.0, 0.0).astype(jnp.bfloat16)
    listed = jnp.concatenate([fact_refs[0][...] * MAP_DEV + fact_refs[1][...], fact_refs[3][...]], axis=0)
    listed = jnp.concatenate([listed.astype(jnp.float32), jnp.zeros((2, LANES - tile_count), jnp.float32)], axis=1)
    listed = jnp.concatenate([listed, jnp.zeros((FACTS - 2, LANES), jnp.float32)], axis=0)
    facts_ref[...] = jnp.dot(listed.astype(jnp.bfloat16), moving, preferred_element_type=jnp.float32)[:2]
    position = lax.broadcasted_iota(jnp.int32, (1, taps), 1)
    a_iota = lax.broadcasted_iota(jnp.int32, (rows, rows), 0)
    b_iota = lax.broadcasted_iota(jnp.int32, (rows, rows), 1)
    tap_at = b_iota - a_iota + taps // 2
    inside = jnp.logical_and(tap_at >= 0, tap_at < taps)

    def toeplitz(d, which):
        kept = jnp.where(position < len_ref[d], taps_ref[which, pl.ds(d, 1), :], 0.0)
        rolled = pltpu.roll(jnp.broadcast_to(kept, (rows, taps)), taps // 2, 1, stride=1, stride_axis=0)
        return jnp.where(inside, jnp.concatenate([rolled] * (rows // taps), axis=1), 0.0)

    for h in range(PHASES):
        for d in range(dates_here):
            if h == 0:
                t_re, t_im = toeplitz(d, 0), toeplitz(d, 1)
                operator_ref[d] = jnp.concatenate(
                    [jnp.concatenate([t_re, -t_im], axis=1), jnp.concatenate([t_im, t_re], axis=1)], axis=0
                ).astype(jnp.bfloat16)
            side = slice(h * LANES, (h + 1) * LANES)
            columns = jnp.concatenate([radar_ref[0, d, :, side], radar_ref[1, d, :, side]], axis=0)
            product = jnp.dot(operator_ref[d], columns, preferred_element_type=jnp.float32)
            for p in range(n):
                for part in range(2):
                    top = part * rows + p * PATCH_AZ
                    cell_ref[p, pl.ds(part * PATCH_AZ * dates_here + d, PATCH_AZ, stride=dates_here), :] = product[
                        top : top + PATCH_AZ
                    ]
        if h == 0:
            for p in range(n):
                cells_ref[p] = cell_ref[p].astype(jnp.bfloat16)

            def first(ks):
                for k in ks:
                    send(facts_ref, got_facts.at[me], fact_send.at[0], fact_recv.at[0], partner(k))
                    send(cells_ref.at[partner(k)], got_cells.at[me], cell_send.at[0], cell_recv.at[0], partner(k))

            got_facts[me] = facts_ref[...]

            @pl.when(middle)
            def _():
                pl.semaphore_wait(barrier, len(close) + len(beside))
                tell(ready_sem, 3 * quarter)
                first(beside)
                pl.semaphore_wait(ready_sem, 1)
                tell(ready_sem, quarter)
                first([k for pair in zip(apart, close[quarter - 1 :][::-1]) for k in pair])
                first(close[: quarter - 1])

            @pl.when(jnp.logical_not(middle))
            def _():
                pl.semaphore_wait(barrier, len(close))
                pl.semaphore_wait(ready_sem, 1)
                first(peers)

            own[0].start()
        else:
            low = lax.broadcasted_iota(jnp.int32, (PATCH_AZ * dates_here, LANES), 1) < LANES // 2
            for p in range(n):
                lines = cell_ref[p].reshape(PATCH_AZ, 2, dates_here, LANES)
                even, odd = [lines[:, i].reshape(PATCH_AZ * dates_here, LANES) for i in range(2)]
                split_ref[0, p] = jnp.where(low, even, pltpu.roll(odd, LANES // 2, 1)).astype(jnp.bfloat16)
                split_ref[1, p] = jnp.where(low, pltpu.roll(even, LANES // 2, 1), odd).astype(jnp.bfloat16)
            for u in range(2):
                for k in peers:
                    send(
                        split_ref.at[u, partner(k)], got_split.at[u, me], cell_send.at[1], cell_recv.at[1 + u], partner(k)
                    )
                own[1 + u].start()

    turned = lax.broadcasted_iota(jnp.int32, (TILE, TILE), 0) - lax.broadcasted_iota(jnp.int32, (TILE, TILE), 1) + TILE
    for t in range(tile_count):
        shift = fact_refs[2][:, t : t + 1]
        step = (turned - shift) & (TILE - 1)
        circ = jnp.zeros((TILE, TILE), jnp.float32)
        for k in range(KW):
            circ = jnp.where(step == k, kern_ref[k], circ)
        shift_ref[t] = circ.astype(jnp.bfloat16)

    def send_rows(q):
        for k in inner:
            to = partner(k) % near
            send(row_msg.at[1, to, q], got_rows.at[1, rank, q], row_send.at[0], row_recv.at[1 + q], partner(k))

    def send_sums(q, ks):
        for k in ks:
            send(sum_msg.at[q, partner(k)], got_sums.at[q, me], sum_send.at[0], sum_recv.at[q], partner(k))

    def send_wide(h, ks):
        for k in ks:
            send(wide_msg.at[h, partner(k)], got_wide.at[h, me], wide_send.at[0], wide_recv.at[h], partner(k))

    def settle():
        drain(got_facts.at[pl.ds(0, n - 1)], fact_recv.at[0])
        from_at = lax.broadcasted_iota(jnp.int32, (tiles, slots), 0)
        into_at = lax.broadcasted_iota(jnp.int32, (tiles, slots), 1)
        twice = ((into_at >> 4) * PATCH_AZ + (into_at & (PATCH_AZ - 1))) == from_at
        twice = jnp.where(twice, 1.0, 0.0).astype(jnp.bfloat16)

        def all_of(k):
            facts = got_facts[k * near]
            for s in range(1, near):
                facts = facts + got_facts[k * near + s]
            return facts

        row_at = lax.broadcasted_iota(jnp.int32, spread_ref.shape[1:], 0)
        slot_at = lax.broadcasted_iota(jnp.int32, spread_ref.shape[1:], 1)
        named = ((row_at >> 4) * MAP_DEV + (row_at & 7)).astype(jnp.float32)
        for k in range(GROUPS):
            here = jnp.concatenate([all_of(k), jnp.zeros((FACTS - 2, tiles), jnp.float32)], axis=0)
            here = jnp.dot(here.astype(jnp.bfloat16), twice, preferred_element_type=jnp.float32)
            same = jnp.logical_and(named == here[0:1], ((row_at ^ slot_at) & PATCH_AZ) == 0)
            spread_ref[k] = jnp.where(same, here[1:2], 0.0).astype(jnp.bfloat16)
        mine = (me * MAP_DEV + lax.broadcasted_iota(jnp.int32, (MAP_DEV, tiles), 0)).astype(jnp.float32)
        count = jnp.zeros((MAP_DEV, tiles), jnp.float32)
        for k in range(GROUPS):
            facts = all_of(k)
            count = count + jnp.where(mine == facts[0:1], facts[1:2], 0.0)
        inv_ref[...] = jnp.broadcast_to(1.0 / jnp.maximum(jnp.sum(count, axis=1, keepdims=True), 1.0), inv_ref.shape)

    def whiten(i, carry):
        whiten_windows(z_ref, i * TOGETHER, white_ref, *work)
        return carry

    def line_of(at):
        return jnp.concatenate([cell_ref[s, at, :] for s in range(n)], axis=0).T.astype(jnp.bfloat16)

    for h in range(PHASES):
        if h == 0:
            own[0].wait()
            drain(got_cells.at[pl.ds(0, n - 1)], cell_recv.at[0])
            for s in range(n):
                cell_ref[s] = got_cells[s].astype(jnp.float32)
            for part in range(2):
                for a in range(PATCH_AZ):
                    line = line_of(pl.ds((part * PATCH_AZ + a) * dates_here, dates_here))
                    for j in range(windows):
                        z_ref[j, a * PATCH_RG : (a + 1) * PATCH_RG, part * total : (part + 1) * total] = line[
                            j * PATCH_RG : (j + 1) * PATCH_RG
                        ]
            lax.fori_loop(0, windows // TOGETHER, whiten, 0)
        else:
            for u in range(2):
                own[1 + u].wait()
                drain(got_split.at[u, pl.ds(0, n - 1)], cell_recv.at[1 + u])
                if u == 1:
                    send_wide(0, range(n - 1, 0, -1))
                for s in range(n):
                    cell_ref[s, : PATCH_AZ * dates_here] = got_split[u, s].astype(jnp.float32)
                for part in range(2):
                    for b in range(PATCH_AZ // 2):
                        line = line_of(pl.ds((part * (PATCH_AZ // 2) + b) * dates_here, dates_here))
                        for i in range(2):
                            a = 2 * b + i
                            for j in range(windows // 2):
                                at = i * (LANES // 2) + j * PATCH_RG
                                z_ref[
                                    u * (windows // 2) + j,
                                    a * PATCH_RG : (a + 1) * PATCH_RG,
                                    part * total : (part + 1) * total,
                                ] = line[at : at + PATCH_RG]
                for i in range(windows // 2 // TOGETHER):
                    whiten(u * (windows // 2 // TOGETHER) + i, 0)

        for a in range(PATCH_AZ):
            flat_ref[pl.ds(a, 2 * total, stride=PATCH_AZ), :] = across(white_ref[a], shift_ref[a * 2 + h])
        for o in range(n):
            wide_msg[h, o] = flat_ref[pl.ds(o * WIDE * PATCH_AZ, WIDE * PATCH_AZ), :].astype(jnp.bfloat16)
        got_wide[h, me] = wide_msg[h, me]
        for q in range(CHUNKS):
            for to in range(near):
                row_msg[h, to, q] = flat_ref[
                    pl.ds((start + (to * CHUNKS + q) * deep) * PATCH_AZ, deep * PATCH_AZ), :
                ].astype(jnp.bfloat16)
            got_rows[h, rank, q] = row_msg[h, rank, q]
            if h == PHASES - 1 and q < AHEAD:
                send_rows(q)
                if q == 0:
                    send_wide(1, range(n - 1, 0, -1))
        if h < PHASES - 1:
            for k in inner:
                to = partner(k) % near
                send(row_msg.at[h, to], got_rows.at[h, rank], row_send.at[0], row_recv.at[0], partner(k))
            settle()

    drain(got_rows.at[0, pl.ds(0, near - 1)], row_recv.at[0])

    def reduce(q, carry):
        drain(got_rows.at[1, pl.ds(0, near - 1), q], row_recv.at[1 + q])
        for i in range(deep // 2):
            at = slice(i * PAIR, (i + 1) * PAIR)
            cells = jnp.concatenate([got_rows[h, s, q, at, :] for h in range(PHASES) for s in range(near)], axis=0)
            out = jnp.dot(spread_ref[group], cells, preferred_element_type=jnp.float32).astype(jnp.bfloat16)
            for o in range(n):
                sum_msg[q, o, at, :] = out[o * PAIR : (o + 1) * PAIR]
        got_sums[q, me] = sum_msg[q, me]
        send_sums(q, range(near, n))

        @pl.when(q + AHEAD < CHUNKS)
        def _():
            send_rows(q + AHEAD)

        send_sums(q, inner)
        return carry

    def whole():
        for h in range(PHASES):
            drain(got_wide.at[h, pl.ds(0, n - 1)], wide_recv.at[h])
        for i in range(WIDE // 2):
            at = slice(i * PAIR, (i + 1) * PAIR)
            out = jnp.zeros((n * PAIR, LANES), jnp.float32)
            for k in range(GROUPS):
                cells = jnp.concatenate(
                    [got_wide[h, k * near + s, at, :] for h in range(PHASES) for s in range(near)], axis=0
                )
                out = out + jnp.dot(spread_ref[k], cells, preferred_element_type=jnp.float32)
            for o in range(n):
                full_msg[o, at, :] = out[o * PAIR : (o + 1) * PAIR].astype(jnp.bfloat16)
        got_full[me] = full_msg[me]
        for k in range(n - 1, 0, -1):
            send(full_msg.at[partner(k)], got_full.at[me], wide_send.at[1], wide_recv.at[PHASES], partner(k))

    lax.fori_loop(0, 2, reduce, 0)
    whole()
    lax.fori_loop(2, CHUNKS, reduce, 0)

    def finish(q, carry):
        drain(got_sums.at[q, pl.ds(0, n - 1)], sum_recv.at[q])

        for s in range(near):
            y = got_sums[q, s].astype(jnp.float32)
            for k in range(1, GROUPS):
                y = y + got_sums[q, s + k * near].astype(jnp.float32)
            for r in range(deep):
                at = pl.ds(start + (s * CHUNKS + q) * deep + r, MAP_DEV, stride=2 * total)
                result_ref[at, :] = y[r * MAP_DEV : (r + 1) * MAP_DEV] * inv_ref[...]
        return carry

    lax.fori_loop(0, CHUNKS - 1, finish, 0)
    drain(got_full.at[pl.ds(0, n - 1)], wide_recv.at[PHASES])
    for s in range(n):
        y = got_full[s].astype(jnp.float32)
        for r in range(WIDE):
            at = pl.ds(s * WIDE + r, MAP_DEV, stride=2 * total)
            result_ref[at, :] = y[r * MAP_DEV : (r + 1) * MAP_DEV] * inv_ref[...]
    finish(CHUNKS - 1, 0)

    drain(got_facts.at[pl.ds(0, n - 1)], fact_send.at[0])
    drain(cells_ref.at[pl.ds(0, n - 1)], cell_send.at[0])
    drain(split_ref.at[:, pl.ds(0, n - 1)], cell_send.at[1])
    drain(row_msg.at[:, pl.ds(0, near - 1)], row_send.at[0])
    drain(sum_msg.at[:, pl.ds(0, n - 1)], sum_send.at[0])
    drain(wide_msg.at[:, pl.ds(0, n - 1)], wide_send.at[0])
    drain(full_msg.at[pl.ds(0, n - 1)], wide_send.at[1])


def shards(n, radar_stack, filter_taps, filter_lengths, resample_kernel, tile_owner, map_slot, correlation, offsets):
    dates_here, rows, ranges = radar_stack.shape[1:]
    dates = n * dates_here
    tile_count = tile_owner.shape[0]
    near = n // GROUPS
    slots = PHASES * near * PAIR
    deep = (2 * dates - n * WIDE) // near // CHUNKS
    block = (n, 2 * PATCH_AZ * dates_here, LANES)
    split = (2, n, PATCH_AZ * dates_here, LANES)
    row_block = (PHASES, near, CHUNKS, deep * PATCH_AZ, LANES)
    sum_block = (CHUNKS, n, MAP_DEV * deep, LANES)
    facts = [x.reshape(1, tile_count) for x in (tile_owner, map_slot, offsets, correlation)]
    given = (filter_lengths, resample_kernel, radar_stack, filter_taps, *facts)

    dma = pltpu.SemaphoreType.DMA
    result = pl.pallas_call(
        partial(flow_kernel, n),
        out_shape=jax.ShapeDtypeStruct((MAP_DEV * 2 * dates, TILE), jnp.float32),
        in_specs=[HBM] * len(given),
        out_specs=VMEM,
        scratch_shapes=[
            pltpu.VMEM(block, jnp.bfloat16),
            pltpu.VMEM(block, jnp.bfloat16),
            pltpu.VMEM(split, jnp.bfloat16),
            pltpu.VMEM(split, jnp.bfloat16),
            pltpu.VMEM((2, slots // 2), jnp.float32),
            pltpu.VMEM((n, 2, slots // 2), jnp.float32),
            pltpu.VMEM(block, jnp.float32),
            pltpu.VMEM((LANES // PATCH_RG, LANES, 2 * dates), jnp.bfloat16),
            pltpu.VMEM((PATCH_AZ, LANES, 2 * dates), jnp.bfloat16),
            pltpu.VMEM((2 * dates * PATCH_AZ, LANES), jnp.float32),
            pltpu.VMEM(row_block, jnp.bfloat16),
            pltpu.VMEM(row_block, jnp.bfloat16),
            pltpu.VMEM(sum_block, jnp.bfloat16),
            pltpu.VMEM(sum_block, jnp.bfloat16),
            pltpu.VMEM((dates_here, 2 * rows, 2 * rows), jnp.bfloat16),
            pltpu.VMEM((GROUPS, n * PAIR, slots), jnp.bfloat16),
            pltpu.VMEM((tile_count, TILE, TILE), jnp.bfloat16),
            pltpu.VMEM((MAP_DEV, LANES), jnp.float32),
            pltpu.VMEM((PHASES, n, WIDE * PATCH_AZ, LANES), jnp.bfloat16),
            pltpu.VMEM((PHASES, n, WIDE * PATCH_AZ, LANES), jnp.bfloat16),
            pltpu.VMEM((n, WIDE * MAP_DEV, LANES), jnp.bfloat16),
            pltpu.VMEM((n, WIDE * MAP_DEV, LANES), jnp.bfloat16),
            pltpu.VMEM((TOGETHER, dates, 2 * dates), jnp.float32),
            pltpu.VMEM((TOGETHER, LANES, 2 * dates), jnp.float32),
            pltpu.VMEM((TOGETHER, dates + LANES, 2 * dates), jnp.bfloat16),
            pltpu.VMEM((TOGETHER, 2 * dates, 2 * dates), jnp.bfloat16),
            pltpu.SMEM(filter_lengths.shape, jnp.int32),
            pltpu.SMEM(resample_kernel.shape, jnp.float32),
            pltpu.VMEM(radar_stack.shape, radar_stack.dtype),
            pltpu.VMEM(filter_taps.shape, jnp.float32),
            pltpu.VMEM((1, tile_count), jnp.int32),
            pltpu.VMEM((1, tile_count), jnp.int32),
            pltpu.VMEM((1, tile_count), jnp.int32),
            pltpu.VMEM((1, tile_count), jnp.int32),
            dma((3,)),
            dma((1,)),
            dma((1,)),
            dma((2,)),
            dma((3,)),
            dma((1,)),
            dma((1 + CHUNKS,)),
            dma((1,)),
            dma((CHUNKS,)),
            dma((2,)),
            dma((PHASES + 1,)),
            dma((len(given),)),
            pltpu.SemaphoreType.REGULAR,
        ],
        compiler_params=pltpu.CompilerParams(collective_id=0, has_side_effects=True, vmem_limit_bytes=BIG),
        name="flow",
    )(*[pltpu.with_memory_space_constraint(x, pltpu.MemorySpace.HBM) for x in given])
    return result.reshape(MAP_DEV, 2 * dates, TILE)


def solution(mesh):
    in_specs = (
        P(None, "date", "grp", None),
        P(None, "date", None),
        P("date"),
        P(),
        P(("grp", "date"), None),
        P(("grp", "date")),
        P(("grp", "date")),
        P(("grp", "date")),
    )
    out_specs = P(("grp", "date"), None, None)
    return jax.shard_map(
        partial(shards, mesh.shape["date"]), mesh=mesh, in_specs=in_specs, out_specs=out_specs, check_vma=False
    )
```
